512 devices in a mesh: blk: 64 (over z, y_lo, core), rep: 8 (over y_hi, x).
Axes of the slice: x: 4, y: 8 (y_hi: 2, y_lo: 4; y = y_hi * 4 + y_lo), z: 8, core: 2. Of those that a mesh axis runs over, the one named last changes fastest.
Arguments:
- points: float32 [16, 81920], P(None, ('blk', 'rep')), may hold values from -3 to 3
- vectors: float32 [32, 81920], P(None, ('blk', 'rep')), may hold values from -1.2 to 1.2
- lengthscales: float32 [16], replicated, may hold values from 0.6 to 1.6
Outputs:
- product: float32 [32, 81920], P(None, ('blk', 'rep'))
The draws below stay inside these ranges and needn't reach their ends.
All inputs are finite; a program needn't handle non-finite values.
Results may differ from the reference program's by a relative error of at most 0.0003.
Values sent between devices are 32-bit elements; how exact they have to be, the bound alone decides.
A program may use at most 64 MiB of HBM per device.

```python
import math
import jax
import jax.numpy as jnp
from jax import lax

FEAT = 16
NVEC = 32
NPTS = 81920


def draw_points(key, part):
    clusters = max(NPTS // 128, 1)
    base = jax.random.fold_in(key, 7301)
    key_member, key_centre, key_spread, key_noise = jax.random.split(base, 4)
    membership = jax.random.randint(key_member, (NPTS,), 0, clusters)
    centres = 0.55 * jax.random.normal(key_centre, (FEAT, clusters), jnp.float32)
    spread = jnp.exp(jax.random.uniform(key_spread, (clusters,), jnp.float32, math.log(0.1), math.log(0.2)))
    noise = jax.random.normal(key_noise, (FEAT, NPTS), jnp.float32)
    placed = jnp.take(centres, membership, axis=1) + jnp.take(spread, membership)[None, :] * noise
    return jnp.clip(placed, -3.0, 3.0)


def draw_lengthscales(key, part):
    base = jax.random.fold_in(key, 5113)
    raw = jnp.exp(jax.random.uniform(base, (FEAT,), jnp.float32, math.log(0.6), math.log(1.6)))
    return jnp.clip(raw, 0.6, 1.6)


def shard_levels(stream_key, dims, pieces, smallest, high):
    def one(position, parts):
        draws = jax.random.uniform(jax.random.fold_in(jax.random.fold_in(stream_key, 6), position), (parts,), jnp.float32, smallest / len(pieces), high / len(pieces))
        return jnp.repeat(jnp.exp(draws), dims[position] // parts).reshape((-1,) + (1,) * (len(dims) - position - 1))

    gain = one(*pieces[0])
    for cut in pieces[1:]:
        gain = gain * one(*cut)
    return gain


def bell_draw(key, shape, deviation, most, cuts=(), held_as=jnp.bfloat16):
    level = shard_levels(key, shape, cuts, -0.22, 0.18) if cuts else 1.0
    result = jax.random.normal(key, shape, jnp.float32) * deviation * level
    return jnp.minimum(jnp.maximum(result, -most), most).astype(held_as)


def setup_inputs(seed: int = 0) -> dict:
    arg_keys = jax.random.split(jax.random.key(seed), 4)
    return {
        "points": draw_points(jax.random.fold_in(arg_keys[3], 71), 0),
        "vectors": bell_draw(arg_keys[1], (NVEC, NPTS), 0.2, 1.2, ((1, 512),), jnp.float32),
        "lengthscales": draw_lengthscales(jax.random.fold_in(arg_keys[3], 71), 0),
    }


def matern_block(row_z, row_sq, all_z, all_sq):
    cross = lax.dot_general(row_z, all_z, (((0,), (0,)), ((), ())), precision=lax.Precision.HIGHEST, preferred_element_type=jnp.float32)
    sqdist = jnp.maximum(row_sq[:, None] + all_sq[None, :] - 2.0 * cross, 0.0)
    svalue = jnp.sqrt(5.0 * sqdist)
    return (1.0 + svalue + svalue * svalue / 3.0) * jnp.exp(-svalue)

def reference(points, vectors, lengthscales):
    scaled = points / lengthscales[:, None]
    squares = lax.optimization_barrier(jnp.sum(scaled * scaled, axis=0))
    total = scaled.shape[1]
    width = math.gcd(total, 512)
    count = total // width

    def one_block(index):
        start = (index * width).astype(jnp.int32)
        row_z = lax.dynamic_slice_in_dim(scaled, start, width, 1)
        row_sq = lax.dynamic_slice_in_dim(squares, start, width, 0)
        kernel = matern_block(row_z, row_sq, scaled, squares)
        return lax.dot_general(vectors, kernel, (((1,), (1,)), ((), ())), precision=lax.Precision.HIGHEST, preferred_element_type=jnp.float32)
    blocks = lax.map(one_block, jnp.arange(count, dtype=jnp.int32))
    return jnp.transpose(blocks, (1, 0, 2)).reshape(vectors.shape[0], total)
```

```python
import functools
import math
import jax
import jax.numpy as jnp
from jax import lax
from jax.experimental import pallas as pl
from jax.experimental.pallas import tpu as pltpu
from jax.sharding import PartitionSpec as P

F = jnp.float32
H = jnp.bfloat16
LN2 = math.log(2.0)
ALPHA = 1.5 / LN2
BETA = 0.75 / (LN2 * LN2)
SCALE = math.sqrt(5.0) / LN2
GAIN = (LN2 * LN2 / 3.0) * 2.0**ALPHA
TINY = 1e-30
TJ, TI = 256, 512

SYM = [(0, 1), (1, 0), (0, 2), (1, 1), (-1, 1), (0, 3), (1, 2), (-1, 2), (1, 3), (-1, 3), (2, 1), (2, 2), (2, 3), (-1, 4)]
OWN = [(0, 0), (2, 0), (0, 4), (2, 4)]
COLS = SYM + OWN
NROW, NCOL, NSYM = 16, len(COLS), len(SYM)
CHUNK_I = NROW + NROW // 4
CHUNK_S = NSYM + -(-NSYM // 4)
CHUNK_O = len(OWN) + -(-len(OWN) // 4) + 1
NI, NJ = CHUNK_I * 128, (CHUNK_S + CHUNK_O) * 128


def split3(value):
    first = value.astype(H).astype(F)
    rest = value - first
    second = rest.astype(H).astype(F)
    return first, second, rest - second


def stacked(*rows):
    index = lax.broadcasted_iota(jnp.int32, (16, 128), 0)
    out = jnp.zeros((16, 128), F)
    for k, value in enumerate(rows):
        out = jnp.where(index == k, value, out)
    return out


def pieces(z, row_side):
    square = jnp.sum(z * z, axis=0, keepdims=True)
    n1, n2, n3 = split3(square)
    x1, x2, x3 = split3(z)
    one, zero = jnp.ones_like(square), jnp.zeros((16, 128), F)
    if row_side:
        parts = [x1, x2, x1, x2, x3, x1, stacked(n1, n2, n3, one, one, one), zero]
    else:
        x1, x2, x3 = -2.0 * x1, -2.0 * x2, -2.0 * x3
        parts = [x1, x1, x2, x2, x1, x3, stacked(one, one, one, n1, n2, n3), zero]
    return jnp.concatenate(parts, axis=0)


def lanes(chunk):
    if isinstance(chunk, int):
        return pl.ds(128 * chunk, 128)
    return pl.ds(pl.multiple_of(chunk * 128, 128), 128)


def put(chunk, z, v, row_side, pts, vec):
    wide = pieces(z, row_side)
    if row_side:
        pts[:, lanes(chunk)] = wide.astype(H)
    else:
        pts[lanes(chunk), :] = wide.T.astype(H)
    high = v.astype(H)
    vec[0:32, lanes(chunk)] = high
    vec[32:64, lanes(chunk)] = (v - high.astype(F)).astype(H)


def prepare(src, first, count, chunk0, row_side, pts, vec):
    @pl.loop(0, count)
    def _(s):
        put(s + chunk0, src[first + s, 0:16, :], src[first + s, 16:48, :], row_side, pts, vec)

    group_of = lax.broadcasted_iota(jnp.int32, (16, 128), 1) // 32
    for g in range(-(-count // 4)):
        outs = [jnp.zeros((16, 128), F) for _ in range(3)]
        for k in range(min(4, count - 4 * g)):
            rem = src[first + 4 * g + k, 48:64, :]
            for q in range(3):
                turn = (32 * (k - q)) % 128
                outs[q] = jnp.where(group_of == k, pltpu.roll(rem, turn, 1) if turn else rem, outs[q])
        put(chunk0 + count + g, outs[0], jnp.concatenate(outs[1:], axis=0), row_side, pts, vec)


def finish(acc, chunk0, count, out, first):
    group_of = lax.broadcasted_iota(jnp.int32, (8, 128), 1) // 32
    for s in range(count):
        c = lanes(chunk0 + s)
        out[first + s, 0:32, :] = (acc[0:32, c] + acc[32:64, c]) * GAIN
    for g in range(-(-count // 4)):
        c = lanes(chunk0 + count + g)
        t = (acc[0:32, c] + acc[32:64, c]) * GAIN
        for k in range(min(4, count - 4 * g)):
            o = jnp.zeros((8, 128), F)
            for q in range(4):
                turn = (32 * (q - k)) % 128
                piece = t[8 * q : 8 * q + 8, :]
                o = jnp.where(group_of == q, pltpu.roll(piece, turn, 1) if turn else piece, o)
            out[first + 4 * g + k, 32:40, :] = o


def products(A, vj, B, vi, acc_i, acc_j, d0, d1, k0, k1):
    nit = NI // TI
    total = nit * (NJ // TJ)

    def place(t):
        return (
            pl.ds(pl.multiple_of(lax.div(t, nit) * TJ, TJ), TJ),
            pl.ds(pl.multiple_of(lax.rem(t, nit) * TI, TI), TI),
        )

    def distances(t, d):
        sj, si = place(t)
        d[...] = jnp.dot(A[sj, :], B[:, si], preferred_element_type=F)

    def kernel_values(d, k):
        x = jnp.maximum(d[...], TINY)
        u = (-ALPHA) - x * lax.rsqrt(x)
        value = (u * u + BETA) * jnp.exp2(u)
        high = value.astype(H)
        k[0] = high
        k[1] = (value - high.astype(F)).astype(H)

    def accumulate(t, k):
        sj, si = place(t)
        v_j, v_i = vj[:, sj], vi[:, si]
        acc_i[:, si] += jnp.dot(
            jnp.concatenate([v_j, v_j], axis=1), jnp.concatenate([k[0], k[1]], axis=0), preferred_element_type=F
        )
        acc_j[:, sj] += lax.dot_general(
            jnp.concatenate([v_i, v_i], axis=1),
            jnp.concatenate([k[0], k[1]], axis=1),
            (((1,), (1,)), ((), ())),
            preferred_element_type=F,
        )

    distances(0, d0)

    @pl.loop(0, total // 2)
    def _(m):
        a = 2 * m
        accumulate(jnp.maximum(a - 1, 0), k1)
        distances(a + 1, d1)
        kernel_values(d0, k0)
        accumulate(a, k0)
        distances(jnp.minimum(a + 2, total - 1), d0)
        kernel_values(d1, k1)

    accumulate(total - 1, k1)


def solve_kernel(p_ref, v_ref, l_ref, out_ref, R, C, B, vi, A, vj, acc_i, acc_j, d0, d1, k0, k1, oi, oj, gi, gj,
                 rs, rr, cs, cr, ris, rir, cjs, cjr):
    b, r = lax.axis_index("blk"), lax.axis_index("rep")
    core, z, x = lax.rem(b, 2), lax.div(b, 8), lax.rem(r, 4)
    y = lax.div(r, 4) * 4 + lax.rem(lax.div(b, 2), 4)

    def at(dx=0, dy=0, dz=0, dc=0):
        xx, yy, zz = lax.rem(x + dx + 4, 4), lax.rem(y + dy + 8, 8), lax.rem(z + dz + 8, 8)
        cc = 1 - core if dc else core
        return ((zz * 4 + lax.rem(yy, 4)) * 2 + cc, lax.div(yy, 4) * 4 + xx)

    own = R.at[0]
    scaled = p_ref[...] / l_ref[...] * SCALE
    R[0, 0:16, :] = scaled[:, 0:128]
    R[0, 16:48, :] = v_ref[:, 0:128]
    R[0, 48:64, 0:32] = scaled[:, 128:160]
    R[0, 48:64, 32:64] = v_ref[0:16, 128:160]
    R[0, 48:64, 64:96] = v_ref[16:32, 128:160]
    R[0, 48:64, 96:128] = jnp.zeros((16, 32), F)
    C[NSYM] = R[0]

    barrier = pltpu.get_barrier_semaphore()
    near = [at(dc=1), at(dz=1), at(dz=-1), at(dy=1), at(dy=-1), at(dx=1), at(dx=-1)]
    for d in near:
        pl.semaphore_signal(barrier, inc=1, device_id=d, device_id_type=pl.DeviceIdType.MESH)
    pl.semaphore_wait(barrier, len(near))

    def send(source, dest, ss, rsem, where):
        return pltpu.make_async_remote_copy(
            src_ref=source, dst_ref=dest, send_sem=ss, recv_sem=rsem, device_id=where,
            device_id_type=pl.DeviceIdType.MESH,
        )

    row, col = {}, {}
    for dz in range(8):
        for dc in range(2):
            s = 2 * dz + dc
            if s == 0:
                continue
            if dc:
                source, where = R.at[2 * dz], at(dc=1)
            elif dz <= 4:
                source, where = R.at[2 * (dz - 1)], at(dz=-1)
            else:
                source, where = R.at[2 * ((dz + 1) % 8)], at(dz=1)
            row[dz, dc] = send(source, R.at[s], rs.at[s], rr.at[s], where)
    slot = {o: k for k, o in enumerate(COLS)}
    for (dx, dy), s in slot.items():
        if (dx, dy) == (0, 0):
            continue
        if dx == 0:
            prev, where = (0, dy - 1), at(dy=-1)
        elif dx == 1:
            prev, where = (0, dy), at(dx=-1)
        elif dx == -1:
            prev, where = (0, dy), at(dx=1)
        elif dy <= 1:
            prev, where = (1, dy), at(dx=-1)
        else:
            prev, where = (-1, dy), at(dx=1)
        source = own if prev == (0, 0) else C.at[slot[prev]]
        col[dx, dy] = send(source, C.at[s], cs.at[s], cr.at[s], where)

    for t in (col[0, 1], row[1, 0], row[7, 0], col[1, 0], row[0, 1]):
        t.start()
    got_row, got_col = [], []

    def arrive_row(dz, *then):
        row[dz, 0].wait_recv()
        for t in then:
            row[t, 0].start()
        row[dz, 1].start()

    def arrive_col(o, *then):
        col[o].wait_recv()
        for t in then:
            col[t].start()

    arrive_col((0, 1), (0, 2), (1, 1), (-1, 1))
    arrive_row(1, 2)
    arrive_row(7, 6)
    arrive_col((1, 0), (2, 0))
    arrive_col((0, 2), (0, 3), (1, 2), (-1, 2))
    arrive_row(2, 3)
    arrive_row(6, 5)
    arrive_col((1, 1), (2, 1))
    arrive_col((0, 3), (0, 4), (1, 3), (-1, 3))
    arrive_row(3, 4)
    arrive_row(5)
    arrive_col((-1, 2), (2, 2))
    arrive_col((0, 4), (-1, 4))
    arrive_row(4)
    arrive_col((-1, 3), (2, 3))
    arrive_col((-1, 4), (2, 4))
    for o in ((-1, 1), (1, 2), (1, 3), (2, 0), (2, 1), (2, 2), (2, 3), (2, 4)):
        arrive_col(o)
    for dz in range(8):
        row[dz, 1].wait_recv()

    prepare(R, 0, NROW, 0, True, B, vi)
    prepare(C, 0, NSYM, 0, False, A, vj)
    prepare(C, NSYM, len(OWN), CHUNK_S, False, A, vj)
    pad = pl.ds(NJ - 128, 128)
    A[pad, :] = jnp.zeros((128, 128), H)
    vj[:, pad] = jnp.zeros((64, 128), H)
    acc_i[...] = jnp.zeros_like(acc_i)
    acc_j[...] = jnp.zeros_like(acc_j)
    k1[...] = jnp.zeros_like(k1)
    products(A, vj, B, vi, acc_i, acc_j, d0, d1, k0, k1)

    finish(acc_j, 0, NSYM, oj, 0)
    backs = []
    for k, (dx, dy) in enumerate(SYM):
        t = send(oj.at[k], gj.at[k], cjs.at[k], cjr.at[k], at(dx=dx, dy=dy))
        t.start()
        backs.append(t)
    finish(acc_i, 0, NROW, oi, 0)
    for dz in (4, 3, 5, 2, 6, 1, 7, 0):
        for dc in (0, 1):
            if dz == 0 and dc == 0:
                continue
            s, d = 2 * dz + dc, 2 * ((8 - dz) % 8) + dc
            t = send(oi.at[s], gi.at[d], ris.at[d], rir.at[d], at(dz=dz, dc=dc))
            t.start()
            backs.append(t)
    total = oi[0]
    for t in backs:
        t.wait_recv()
    for s in range(1, NROW):
        total = total + gi[s]
    for k in range(NSYM):
        total = total + gj[k]
    out_ref[:, 0:128] = total[0:32]
    rem = total[32:40]
    for q in range(4):
        turned = pltpu.roll(rem, (-32 * q) % 128, 1) if q else rem
        out_ref[8 * q : 8 * q + 8, 128:160] = turned[:, 0:32]
    for t in (*row.values(), *col.values(), *backs):
        t.wait_send()


def per_device(points, vectors, lengthscales):
    vmem = pl.BlockSpec(memory_space=pltpu.VMEM)
    dma = pltpu.SemaphoreType.DMA
    return pl.pallas_call(
        solve_kernel,
        out_shape=jax.ShapeDtypeStruct(vectors.shape, F),
        in_specs=[vmem] * 3,
        out_specs=vmem,
        scratch_shapes=[
            pltpu.VMEM((NROW, 64, 128), F),
            pltpu.VMEM((NCOL, 64, 128), F),
            pltpu.VMEM((128, NI), H),
            pltpu.VMEM((64, NI), H),
            pltpu.VMEM((NJ, 128), H),
            pltpu.VMEM((64, NJ), H),
            pltpu.VMEM((64, NI), F),
            pltpu.VMEM((64, NJ), F),
            pltpu.VMEM((TJ, TI), F),
            pltpu.VMEM((TJ, TI), F),
            pltpu.VMEM((2, TJ, TI), H),
            pltpu.VMEM((2, TJ, TI), H),
            pltpu.VMEM((NROW, 40, 128), F),
            pltpu.VMEM((NSYM, 40, 128), F),
            pltpu.VMEM((NROW, 40, 128), F),
            pltpu.VMEM((NSYM, 40, 128), F),
            dma((NROW,)), dma((NROW,)), dma((NCOL,)), dma((NCOL,)),
            dma((NROW,)), dma((NROW,)), dma((NSYM,)), dma((NSYM,)),
        ],
        compiler_params=pltpu.CompilerParams(collective_id=0, has_side_effects=True),
        name="solve",
    )(points, vectors, lengthscales[:, None])


def solution(mesh):
    return jax.shard_map(
        per_device,
        mesh=mesh,
        in_specs=(P(None, ("blk", "rep")), P(None, ("blk", "rep")), P()),
        out_specs=P(None, ("blk", "rep")),
        check_vma=False,
    )
```

```python
import functools
import math
import jax
import jax.numpy as jnp
from jax import lax
from jax.experimental import pallas as pl
from jax.experimental.pallas import tpu as pltpu
from jax.sharding import PartitionSpec as P

F = jnp.float32
H = jnp.bfloat16
LN2 = math.log(2.0)
ALPHA = 1.5 / LN2
BETA = 0.75 / (LN2 * LN2)
SCALE = math.sqrt(5.0) / LN2
GAIN = (LN2 * LN2 / 3.0) * 2.0**ALPHA
TINY = 1e-30
TILE = 256

ROWS = [0, 1, 7, 2, 6, 3, 5, 4]
SYM = [(0, 1), (1, 0), (0, 2), (1, 1), (-1, 1), (0, 3), (1, 2), (-1, 2), (2, 1), (1, 3), (-1, 3), (2, 2), (2, 3), (-1, 4)]
OWN = [(0, 0), (2, 0), (0, 4), (2, 4)]
COLS = SYM + OWN
NROW, NCOL, NSYM = 16, len(COLS), len(SYM)
CHUNK_S = NSYM + -(-NSYM // 4)
NI, NJ = 128 * (NROW + NROW // 4), 128 * 24


def split3(value):
    first = value.astype(H).astype(F)
    rest = value - first
    second = rest.astype(H).astype(F)
    return first, second, rest - second


def stacked(*rows):
    index = lax.broadcasted_iota(jnp.int32, (16, 128), 0)
    out = jnp.zeros((16, 128), F)
    for k, value in enumerate(rows):
        out = jnp.where(index == k, value, out)
    return out


def pieces(z, row_side):
    square = jnp.sum(z * z, axis=0, keepdims=True)
    n1, n2, n3 = split3(square)
    x1, x2, x3 = split3(z)
    one, zero = jnp.ones_like(square), jnp.zeros((16, 128), F)
    if row_side:
        parts = [x1, x2, x1, x2, x3, x1, stacked(n1, n2, n3, one, one, one), zero]
    else:
        x1, x2, x3 = -2.0 * x1, -2.0 * x2, -2.0 * x3
        parts = [x1, x1, x2, x2, x1, x3, stacked(one, one, one, n1, n2, n3), zero]
    return jnp.concatenate(parts, axis=0)


def lanes(chunk):
    if isinstance(chunk, int):
        return pl.ds(128 * chunk, 128)
    return pl.ds(pl.multiple_of(chunk * 128, 128), 128)


def put(chunk, z, v, row_side, pts, vec):
    wide = pieces(z, row_side)
    if row_side:
        pts[:, lanes(chunk)] = wide.astype(H)
    else:
        pts[lanes(chunk), :] = wide.T.astype(H)
    high = v.astype(H)
    vec[0:32, lanes(chunk)] = high
    vec[32:64, lanes(chunk)] = (v - high.astype(F)).astype(H)


def prepare(src, slots, chunk0, row_side, pts, vec):
    first, count = slots

    @pl.loop(0, count)
    def _(s):
        put(chunk0 + s, src[first + s, 0:16, :], src[first + s, 16:48, :], row_side, pts, vec)


def prepare_rest(src, slots, chunk, row_side, pts, vec):
    first, count = slots
    group_of = lax.broadcasted_iota(jnp.int32, (16, 128), 1) // 32
    outs = [jnp.zeros((16, 128), F) for _ in range(3)]
    for k in range(count):
        rem = src[first + k, 48:64, :]
        for q in range(3):
            turn = (32 * (k - q)) % 128
            outs[q] = jnp.where(group_of == k, pltpu.roll(rem, turn, 1) if turn else rem, outs[q])
    put(chunk, outs[0], jnp.concatenate(outs[1:], axis=0), row_side, pts, vec)


def finish(acc, slots, chunk0, rest, out):
    first, count = slots
    group_of = lax.broadcasted_iota(jnp.int32, (8, 128), 1) // 32
    c = lanes(rest)
    t = (acc[0:32, c] + acc[32:64, c]) * GAIN
    for k in range(count):
        c = lanes(chunk0 + k)
        out[first + k, 0:32, :] = (acc[0:32, c] + acc[32:64, c]) * GAIN
        o = jnp.zeros((8, 128), F)
        for q in range(4):
            turn = (32 * (q - k)) % 128
            piece = t[8 * q : 8 * q + 8, :]
            o = jnp.where(group_of == q, pltpu.roll(piece, turn, 1) if turn else piece, o)
        out[first + k, 32:40, :] = o


def block_of(m):
    late = m - 15
    j = jnp.where(m < 9, lax.div(m, 3), jnp.where(m < 12, m - 9, jnp.where(m < 15, m - 12, jnp.where(m < 25, 3 + lax.div(jnp.maximum(late, 0), 5), 5))))
    i = jnp.where(m < 9, lax.rem(m, 3), jnp.where(m < 12, 3, jnp.where(m < 15, 4, jnp.where(m < 25, lax.rem(jnp.maximum(late, 0), 5), 29 - m))))
    return j, i


STEPS = 30


def products(A, vj, B, vi, acc_i, acc_j, d, k, actions):
    def place(block, q):
        j, i = block
        return (
            pl.ds(pl.multiple_of((2 * j + q // 2) * TILE, TILE), TILE),
            pl.ds(pl.multiple_of((2 * i + q % 2) * TILE, TILE), TILE),
        )

    def distances(block, q):
        sj, si = place(block, q)
        d[q][...] = jnp.dot(A[sj, :], B[:, si], preferred_element_type=F)

    def kernel_values(q):
        x = jnp.maximum(d[q][...], TINY)
        u = (-ALPHA) - x * lax.rsqrt(x)
        value = (u * u + BETA) * jnp.exp2(u)
        high = value.astype(H)
        k[q][0] = high
        k[q][1] = (value - high.astype(F)).astype(H)

    def accumulate(block, q):
        sj, si = place(block, q)
        v_j, v_i = vj[:, sj], vi[:, si]
        acc_i[:, si] += jnp.dot(
            jnp.concatenate([v_j, v_j], axis=1), jnp.concatenate([k[q][0], k[q][1]], axis=0), preferred_element_type=F
        )
        acc_j[:, sj] += jnp.dot(
            jnp.concatenate([v_i, v_i], axis=1), jnp.concatenate([k[q][0].T, k[q][1].T], axis=0), preferred_element_type=F
        )

    for q in range(3):
        distances(block_of(jnp.int32(0)), q)
    for q in range(1, 4):
        k[q][...] = jnp.zeros_like(k[q])

    @pl.loop(0, STEPS)
    def _(m):
        for step, action in actions.items():
            if step < STEPS:
                pl.when(m == step)(action)
        before, now = block_of(jnp.maximum(m - 1, 0)), block_of(m)
        after = block_of(jnp.minimum(m + 1, STEPS - 1))
        for q in range(4):
            distances(after if q else now, (q + 3) % 4)
            accumulate(before if q < 3 else now, (q + 1) % 4)
            kernel_values(q)

    actions[STEPS]()
    for q in range(1, 4):
        accumulate(block_of(jnp.int32(STEPS - 1)), q)


def solve_kernel(p_hbm, v_hbm, l_ref, out_ref, p_ref, v_ref, R, C, B, vi, A, vj, acc_i, acc_j, d0, d1, d2, d3, k0, k1, k2, k3,
                 oi, oj, gi, gj, io, rs, rr, cs, cr, ris, rir, cjs, cjr):
    b, r = lax.axis_index("blk"), lax.axis_index("rep")
    core, z, x = lax.rem(b, 2), lax.div(b, 8), lax.rem(r, 4)
    y = lax.div(r, 4) * 4 + lax.rem(lax.div(b, 2), 4)

    def at(dx=0, dy=0, dz=0, dc=0):
        xx, yy, zz = lax.rem(x + dx + 4, 4), lax.rem(y + dy + 8, 8), lax.rem(z + dz + 8, 8)
        cc = 1 - core if dc else core
        return ((zz * 4 + lax.rem(yy, 4)) * 2 + cc, lax.div(yy, 4) * 4 + xx)

    barrier = pltpu.get_barrier_semaphore()
    near = [at(dc=1), at(dz=1), at(dz=-1), at(dy=1), at(dy=-1), at(dx=1), at(dx=-1)]
    for d in near:
        pl.semaphore_signal(barrier, inc=1, device_id=d, device_id_type=pl.DeviceIdType.MESH)
    loads = [pltpu.make_async_copy(p_hbm, p_ref, io.at[0]), pltpu.make_async_copy(v_hbm, v_ref, io.at[1])]
    for t in loads:
        t.start()
    feature = lax.broadcasted_iota(jnp.int32, (16, 160), 0)
    scale = jnp.ones((16, 160), F)
    for f in range(16):
        scale = jnp.where(feature == f, l_ref[f], scale)
    acc_i[...] = jnp.zeros_like(acc_i)
    acc_j[...] = jnp.zeros_like(acc_j)
    pad = pl.ds(NJ - 128, 128)
    A[pad, :] = jnp.zeros((128, 128), H)
    vj[:, pad] = jnp.zeros((64, 128), H)
    for t in loads:
        t.wait()

    own = R.at[0]
    scaled = p_ref[...] / scale * SCALE
    R[0, 0:16, :] = scaled[:, 0:128]
    R[0, 16:48, :] = v_ref[:, 0:128]
    R[0, 48:64, 0:32] = scaled[:, 128:160]
    R[0, 48:64, 32:64] = v_ref[0:16, 128:160]
    R[0, 48:64, 64:96] = v_ref[16:32, 128:160]
    R[0, 48:64, 96:128] = jnp.zeros((16, 32), F)
    C[NSYM] = R[0]
    pl.semaphore_wait(barrier, len(near))

    def send(source, dest, ss, rsem, where):
        return pltpu.make_async_remote_copy(
            src_ref=source, dst_ref=dest, send_sem=ss, recv_sem=rsem, device_id=where,
            device_id_type=pl.DeviceIdType.MESH,
        )

    row, col = {}, {}
    rslot = {dz: 2 * k for k, dz in enumerate(ROWS)}
    for dz in range(8):
        for dc in range(2):
            s = rslot[dz] + dc
            if s == 0:
                continue
            if dc:
                source, where = R.at[rslot[dz]], at(dc=1)
            elif dz <= 4:
                source, where = R.at[rslot[dz - 1]], at(dz=-1)
            else:
                source, where = R.at[rslot[(dz + 1) % 8]], at(dz=1)
            row[dz, dc] = send(source, R.at[s], rs.at[s], rr.at[s], where)
    slot = {o: k for k, o in enumerate(COLS)}
    for (dx, dy), s in slot.items():
        if (dx, dy) == (0, 0):
            continue
        if dx == 0:
            prev, where = (0, dy - 1), at(dy=-1)
        elif dx == 1:
            prev, where = (0, dy), at(dx=-1)
        elif dx == -1:
            prev, where = (0, dy), at(dx=1)
        elif dy <= 1:
            prev, where = (1, dy), at(dx=-1)
        else:
            prev, where = (-1, dy), at(dx=1)
        source = own if prev == (0, 0) else C.at[slot[prev]]
        col[dx, dy] = send(source, C.at[s], cs.at[s], cr.at[s], where)

    for t in (col[0, 1], row[1, 0], row[7, 0], col[1, 0], row[0, 1]):
        t.start()

    def arrive_row(dz, *then):
        row[dz, 0].wait_recv()
        for t in then:
            row[t, 0].start()
        row[dz, 1].start()

    def arrive_col(o, *then):
        col[o].wait_recv()
        for t in then:
            col[t].start()

    def rows_ready(*offsets):
        for dz in offsets:
            row[dz, 1].wait_recv()

    def prepare_rows(group):
        prepare(R, (4 * group, 4), 4 * group, True, B, vi)

    def prepare_cols(first, count, chunk):
        prepare(C, (first, count), chunk, False, A, vj)

    backs = {}

    def back(key, source, dest, ss, rsem, where):
        backs[key] = send(source, dest, ss, rsem, where)

    for k, (dx, dy) in enumerate(SYM):
        back((dx, dy), oj.at[k], gj.at[k], cjs.at[k], cjr.at[k], at(dx=dx, dy=dy))
    for dz in range(8):
        for dc in range(2):
            if (dz, dc) != (0, 0):
                s, d = rslot[dz] + dc, rslot[(8 - dz) % 8] + dc
                back((dz, dc, 0), oi.at[s], gi.at[d], ris.at[d], rir.at[d], at(dz=dz, dc=dc))

    def return_rows(group):
        finish(acc_i, (4 * group, 4), 4 * group, NROW + group, oi)
        for k in (2 * group + 1, 2 * group):
            for dc in range(2):
                if (ROWS[k], dc) != (0, 0):
                    backs[ROWS[k], dc, 0].start()

    def return_cols():
        for g in range(4):
            finish(acc_j, (4 * g, min(4, NSYM - 4 * g)), 4 * g, NSYM + g, oj)
        for o in SYM:
            backs[o].start()

    arrive_col((0, 1), (0, 2), (1, 1), (-1, 1))
    arrive_row(1, 2)
    arrive_row(7, 6)
    arrive_col((1, 0), (2, 0))
    arrive_col((0, 2), (0, 3), (1, 2), (-1, 2))
    arrive_row(2, 3)
    arrive_row(6, 5)
    arrive_col((1, 1), (2, 1))
    rows_ready(0, 1)
    prepare_rows(0)
    prepare_cols(0, 4, 0)
    rows_ready(7, 2)
    prepare_rows(1)

    def at_1():
        arrive_col((0, 3), (0, 4), (1, 3), (-1, 3))
        arrive_row(3, 4)
        arrive_row(5)
        rows_ready(6, 3)
        prepare_rows(2)

    def at_2():
        arrive_col((-1, 2), (2, 2))
        arrive_col((-1, 1))
        arrive_col((1, 2))
        prepare_cols(4, 4, 4)

    def at_5():
        arrive_col((0, 4), (-1, 4))
        arrive_row(4)
        arrive_col((-1, 3), (2, 3))
        arrive_col((2, 1))
        arrive_col((1, 3))
        arrive_col((2, 2))
        prepare_cols(8, 4, 8)

    def at_8():
        rows_ready(5, 4)
        prepare_rows(3)

    def at_11():
        for g in range(4):
            prepare_rest(R, (4 * g, 4), NROW + g, True, B, vi)

    def at_14():
        arrive_col((-1, 4), (2, 4))
        arrive_col((2, 3))
        prepare_cols(12, 2, 12)
        for g in range(2):
            prepare_rest(C, (4 * g, 4), NSYM + g, False, A, vj)

    def at_19():
        arrive_col((2, 0))
        for g in range(2, 4):
            prepare_rest(C, (4 * g, min(4, NSYM - 4 * g)), NSYM + g, False, A, vj)
        prepare_cols(NSYM, 2, CHUNK_S)

    def at_24():
        arrive_col((2, 4))
        prepare_cols(NSYM + 2, 2, CHUNK_S + 2)
        prepare_rest(C, (NSYM, 4), CHUNK_S + 4, False, A, vj)

    actions = {
        1: at_1, 2: at_2, 5: at_5, 8: at_8, 11: at_11, 14: at_14, 19: at_19, 24: at_24,
        26: return_cols,
        28: lambda: return_rows(3),
        29: lambda: return_rows(2),
        STEPS: lambda: return_rows(1),
    }
    products(A, vj, B, vi, acc_i, acc_j, (d0, d1, d2, d3), (k0, k1, k2, k3), actions)
    return_rows(0)

    total = oi[0]
    for k, o in enumerate(SYM):
        backs[o].wait_recv()
        total = total + gj[k]
    for dz in (*ROWS[:0:-1], 0):
        for dc in range(2):
            if (dz, dc) != (0, 0):
                backs[dz, dc, 0].wait_recv()
                total = total + gi[rslot[(8 - dz) % 8] + dc]
    out_ref[:, 0:128] = total[0:32]
    rem = total[32:40]
    for q in range(4):
        turned = pltpu.roll(rem, (-32 * q) % 128, 1) if q else rem
        out_ref[8 * q : 8 * q + 8, 128:160] = turned[:, 0:32]
    for t in (*row.values(), *col.values(), *backs.values()):
        t.wait_send()


def per_device(points, vectors, lengthscales):
    vmem = pl.BlockSpec(memory_space=pltpu.VMEM)
    dma = pltpu.SemaphoreType.DMA
    return pl.pallas_call(
        solve_kernel,
        out_shape=jax.ShapeDtypeStruct(vectors.shape, F),
        in_specs=[pl.BlockSpec(memory_space=pl.ANY)] * 2 + [pl.BlockSpec(memory_space=pltpu.SMEM)],
        out_specs=vmem,
        scratch_shapes=[
            pltpu.VMEM(points.shape, F),
            pltpu.VMEM(vectors.shape, F),
            pltpu.VMEM((NROW, 64, 128), F),
            pltpu.VMEM((NCOL, 64, 128), F),
            pltpu.VMEM((128, NI), H),
            pltpu.VMEM((64, NI), H),
            pltpu.VMEM((NJ, 128), H),
            pltpu.VMEM((64, NJ), H),
            pltpu.VMEM((64, NI), F),
            pltpu.VMEM((64, NJ), F),
            *[pltpu.VMEM((TILE, TILE), F)] * 4,
            *[pltpu.VMEM((2, TILE, TILE), H)] * 4,
            pltpu.VMEM((NROW, 40, 128), F),
            pltpu.VMEM((NSYM, 40, 128), F),
            pltpu.VMEM((NROW, 40, 128), F),
            pltpu.VMEM((NSYM, 40, 128), F),
            dma((2,)),
            dma((NROW,)), dma((NROW,)), dma((NCOL,)), dma((NCOL,)),
            dma((NROW,)), dma((NROW,)), dma((NSYM,)), dma((NSYM,)),
        ],
        compiler_params=pltpu.CompilerParams(collective_id=0, has_side_effects=True),
        name="solve",
    )(points, vectors, lengthscales)


def solution(mesh):
    return jax.shard_map(
        per_device,
        mesh=mesh,
        in_specs=(P(None, ("blk", "rep")), P(None, ("blk", "rep")), P()),
        out_specs=P(None, ("blk", "rep")),
        check_vma=False,
    )
```

```python
import functools
import math
import jax
import jax.numpy as jnp
from jax import lax
from jax.experimental import pallas as pl
from jax.experimental.pallas import tpu as pltpu
from jax.sharding import PartitionSpec as P

F = jnp.float32
H = jnp.bfloat16
LN2 = math.log(2.0)
ALPHA = 1.5 / LN2
BETA = 0.75 / (LN2 * LN2)
SCALE = math.sqrt(5.0) / LN2
GAIN = (LN2 * LN2 / 3.0) * 2.0**ALPHA
TINY = 1e-30
TILE = 256

ROWS = [0, 1, 7, 2, 6, 3, 5, 4]
SYM = [(0, 1), (1, 0), (0, 2), (0, 3), (1, 1), (-1, 1), (1, 2), (-1, 2), (2, 1), (2, 2), (1, 3), (-1, 3), (2, 3), (-1, 4)]
OWN = [(0, 0), (2, 0), (0, 4), (2, 4)]
COLS = SYM + OWN
NROW, NCOL, NSYM = 16, len(COLS), len(SYM)
CHUNK_S = NSYM + -(-NSYM // 4)
NI, NJ = 128 * (NROW + NROW // 4), 128 * 24


def split3(value):
    first = value.astype(H).astype(F)
    rest = value - first
    second = rest.astype(H).astype(F)
    return first, second, rest - second


def stacked(*rows):
    index = lax.broadcasted_iota(jnp.int32, (16, 128), 0)
    out = jnp.zeros((16, 128), F)
    for k, value in enumerate(rows):
        out = jnp.where(index == k, value, out)
    return out


def pieces(z, row_side):
    square = jnp.sum(z * z, axis=0, keepdims=True)
    n1, n2, n3 = split3(square)
    x1, x2, x3 = split3(z)
    one, zero = jnp.ones_like(square), jnp.zeros((16, 128), F)
    if row_side:
        parts = [x1, x2, x1, x2, x3, x1, stacked(n1, n2, n3, one, one, one), zero]
    else:
        x1, x2, x3 = -2.0 * x1, -2.0 * x2, -2.0 * x3
        parts = [x1, x1, x2, x2, x1, x3, stacked(one, one, one, n1, n2, n3), zero]
    return jnp.concatenate(parts, axis=0)


def lanes(chunk):
    if isinstance(chunk, int):
        return pl.ds(128 * chunk, 128)
    return pl.ds(pl.multiple_of(chunk * 128, 128), 128)


def put(chunk, z, v, row_side, pts, vec):
    wide = pieces(z, row_side)
    if row_side:
        pts[:, lanes(chunk)] = wide.astype(H)
    else:
        pts[lanes(chunk), :] = wide.T.astype(H)
    high = v.astype(H)
    vec[0:32, lanes(chunk)] = high
    vec[32:64, lanes(chunk)] = (v - high.astype(F)).astype(H)


def prepare(src, slots, chunk0, row_side, pts, vec):
    first, count = slots

    @pl.loop(0, count)
    def _(s):
        put(chunk0 + s, src[first + s, 0:16, :], src[first + s, 16:48, :], row_side, pts, vec)


def prepare_rest(src, slots, chunk, row_side, pts, vec):
    first, count = slots
    group_of = lax.broadcasted_iota(jnp.int32, (16, 128), 1) // 32
    outs = [jnp.zeros((16, 128), F) for _ in range(3)]
    for k in range(count):
        rem = src[first + k, 48:64, :]
        for q in range(3):
            turn = (32 * (k - q)) % 128
            outs[q] = jnp.where(group_of == k, pltpu.roll(rem, turn, 1) if turn else rem, outs[q])
    put(chunk, outs[0], jnp.concatenate(outs[1:], axis=0), row_side, pts, vec)


def finish_main(acc, slots, chunk0, out):
    first, count = slots
    for k in range(count):
        c = lanes(chunk0 + k)
        out[first + k, 0:32, :] = (acc[0:32, c] + acc[32:64, c]) * GAIN


def finish_rest(acc, slots, rest, out):
    first, count = slots
    group_of = lax.broadcasted_iota(jnp.int32, (8, 128), 1) // 32
    c = lanes(rest)
    t = (acc[0:32, c] + acc[32:64, c]) * GAIN
    for k in range(count):
        o = jnp.zeros((8, 128), F)
        for q in range(4):
            turn = (32 * (q - k)) % 128
            piece = t[8 * q : 8 * q + 8, :]
            o = jnp.where(group_of == q, pltpu.roll(piece, turn, 1) if turn else piece, o)
        out[first + k, 32:40, :] = o


def block_of(m):
    def pick(cond, yes, no):
        return jnp.where(cond, yes, no)

    third = pick(m >= 6, 2, pick(m >= 3, 1, 0))
    pair = lax.shift_right_logical(jnp.maximum(m - 20, 0), 1)
    j = pick(m < 9, third, pick(m < 12, m - 9, pick(m < 15, m - 12, pick(m < 20, 3, m - 16 - 2 * pair))))
    i = pick(m < 9, m - 3 * third, pick(m < 12, 3, pick(m < 15, 4, pick(m < 20, m - 15, 4 - pair))))
    return j, i


STEPS = 30


def products(A, vj, B, vi, acc_i, acc_j, d, k, actions):
    def place(block, q):
        j, i = block
        return (
            pl.ds(pl.multiple_of((2 * j + q // 2) * TILE, TILE), TILE),
            pl.ds(pl.multiple_of((2 * i + q % 2) * TILE, TILE), TILE),
        )

    def distances(block, q):
        sj, si = place(block, q)
        d[q][...] = jnp.dot(A[sj, :], B[:, si], preferred_element_type=F)

    def kernel_values(q):
        x = jnp.maximum(d[q][...], TINY)
        u = (-ALPHA) - x * lax.rsqrt(x)
        value = (u * u + BETA) * jnp.exp2(u)
        high = value.astype(H)
        k[q][0] = high
        k[q][1] = (value - high.astype(F)).astype(H)

    def accumulate(block, q):
        sj, si = place(block, q)
        v_j, v_i = vj[:, sj], vi[:, si]
        acc_i[:, si] += jnp.dot(
            jnp.concatenate([v_j, v_j], axis=1), jnp.concatenate([k[q][0], k[q][1]], axis=0), preferred_element_type=F
        )
        acc_j[:, sj] += jnp.dot(
            jnp.concatenate([v_i, v_i], axis=1), jnp.concatenate([k[q][0].T, k[q][1].T], axis=0), preferred_element_type=F
        )

    for q in range(3):
        distances(block_of(jnp.int32(0)), q)
    for q in range(1, 4):
        k[q][...] = jnp.zeros_like(k[q])

    def step(m, blocks):
        for at, action in actions.items():
            if at < STEPS:
                pl.when(m == at)(action)
        before, now, after = blocks
        for q in range(4):
            distances(after if q else now, (q + 3) % 4)
            accumulate(before if q < 3 else now, (q + 1) % 4)
            kernel_values(q)
        return now, after, block_of(jnp.minimum(m + 2, STEPS - 1))

    start = block_of(jnp.int32(0))
    lax.fori_loop(0, STEPS, step, (start, start, block_of(jnp.int32(1))))
    actions[STEPS]()
    for q in range(1, 4):
        accumulate(block_of(jnp.int32(STEPS - 1)), q)


def solve_kernel(p_hbm, v_hbm, l_ref, out_ref, p_ref, v_ref, R, C, B, vi, A, vj, acc_i, acc_j, d0, d1, d2, d3, k0, k1, k2, k3,
                 oi, oj, gi, gj, io, rs, rr, cs, cr, ris, rir, cjs, cjr):
    b, r = lax.axis_index("blk"), lax.axis_index("rep")
    core, z, x = lax.rem(b, 2), lax.div(b, 8), lax.rem(r, 4)
    y = lax.div(r, 4) * 4 + lax.rem(lax.div(b, 2), 4)

    def at(dx=0, dy=0, dz=0, dc=0):
        xx, yy, zz = lax.rem(x + dx + 4, 4), lax.rem(y + dy + 8, 8), lax.rem(z + dz + 8, 8)
        cc = 1 - core if dc else core
        return ((zz * 4 + lax.rem(yy, 4)) * 2 + cc, lax.div(yy, 4) * 4 + xx)

    barrier = pltpu.get_barrier_semaphore()
    near = [at(dc=1)] + [at(dz=k) for k in range(1, 8)] + [at(dy=k) for k in range(1, 8)] + [at(dx=k) for k in range(1, 4)]
    for d in near:
        pl.semaphore_signal(barrier, inc=1, device_id=d, device_id_type=pl.DeviceIdType.MESH)
    loads = [pltpu.make_async_copy(p_hbm, p_ref, io.at[0]), pltpu.make_async_copy(v_hbm, v_ref, io.at[1])]
    for t in loads:
        t.start()
    feature = lax.broadcasted_iota(jnp.int32, (16, 160), 0)
    scale = jnp.ones((16, 160), F)
    for f in range(16):
        scale = jnp.where(feature == f, l_ref[f], scale)
    acc_i[...] = jnp.zeros_like(acc_i)
    acc_j[...] = jnp.zeros_like(acc_j)
    pad = pl.ds(NJ - 128, 128)
    A[pad, :] = jnp.zeros((128, 128), H)
    vj[:, pad] = jnp.zeros((64, 128), H)
    for t in loads:
        t.wait()

    own = R.at[0]
    scaled = p_ref[...] / scale * SCALE
    R[0, 0:16, :] = scaled[:, 0:128]
    R[0, 16:48, :] = v_ref[:, 0:128]
    R[0, 48:64, 0:32] = scaled[:, 128:160]
    R[0, 48:64, 32:64] = v_ref[0:16, 128:160]
    R[0, 48:64, 64:96] = v_ref[16:32, 128:160]
    R[0, 48:64, 96:128] = jnp.zeros((16, 32), F)
    C[NSYM] = R[0]
    pl.semaphore_wait(barrier, len(near))

    def send(source, dest, ss, rsem, where):
        return pltpu.make_async_remote_copy(
            src_ref=source, dst_ref=dest, send_sem=ss, recv_sem=rsem, device_id=where,
            device_id_type=pl.DeviceIdType.MESH,
        )

    row, col = {}, {}
    rslot = {dz: 2 * k for k, dz in enumerate(ROWS)}
    for dz in range(8):
        for dc in range(2):
            s = rslot[dz] + dc
            if s == 0:
                continue
            if dc:
                source, where = R.at[rslot[dz]], at(dc=1)
            else:
                source, where = own, at(dz=-dz)
            row[dz, dc] = send(source, R.at[s], rs.at[s], rr.at[s], where)
    slot = {o: k for k, o in enumerate(COLS)}
    for (dx, dy), s in slot.items():
        if (dx, dy) == (0, 0):
            continue
        if dx == 0:
            prev, where = (0, 0), at(dy=-dy)
        else:
            prev, where = (0, dy), at(dx=-dx)
        source = own if prev == (0, 0) else C.at[slot[prev]]
        col[dx, dy] = send(source, C.at[s], cs.at[s], cr.at[s], where)

    for t in (col[0, 1], row[1, 0], row[7, 0], col[1, 0], row[0, 1], col[0, 2], row[2, 0], row[6, 0], col[2, 0],
              col[0, 3], row[3, 0], row[5, 0], col[0, 4], row[4, 0]):
        t.start()

    def arrive_row(dz, *then):
        row[dz, 0].wait_recv()
        for t in then:
            row[t, 0].start()
        row[dz, 1].start()

    def arrive_col(o, *then):
        col[o].wait_recv()
        for t in then:
            col[t].start()

    def rows_ready(*offsets):
        for dz in offsets:
            row[dz, 1].wait_recv()

    def prepare_rows(group):
        prepare(R, (4 * group, 4), 4 * group, True, B, vi)

    def prepare_cols(first, count, chunk):
        prepare(C, (first, count), chunk, False, A, vj)

    backs = {}

    def back(key, source, dest, ss, rsem, where):
        backs[key] = send(source, dest, ss, rsem, where)

    for k, (dx, dy) in enumerate(SYM):
        for part, rows in enumerate((pl.ds(0, 32), pl.ds(32, 8))):
            e = 2 * k + part
            back((dx, dy, part), oj.at[k, rows], gj.at[k, rows], cjs.at[e], cjr.at[e], at(dx=dx, dy=dy))
    for dz in range(8):
        for dc in range(2):
            if (dz, dc) != (0, 0):
                s, d = rslot[dz] + dc, rslot[(8 - dz) % 8] + dc
                back((dz, dc), oi.at[s], gi.at[d], ris.at[d], rir.at[d], at(dz=dz, dc=dc))

    def return_rows(group):
        finish_main(acc_i, (4 * group, 4), 4 * group, oi)
        finish_rest(acc_i, (4 * group, 4), NROW + group, oi)
        for k in (2 * group + 1, 2 * group):
            for dc in range(2):
                if (ROWS[k], dc) != (0, 0):
                    backs[ROWS[k], dc].start()

    def return_cols(part, first, count):
        for o in SYM[first : first + count]:
            backs[(*o, part)].start()

    def cols_main():
        finish_main(acc_j, (0, 12), 0, oj)
        return_cols(0, 0, 12)

    def cols_next():
        finish_main(acc_j, (12, 2), 12, oj)
        for g in range(2):
            finish_rest(acc_j, (4 * g, 4), NSYM + g, oj)
        return_cols(0, 12, 2)
        return_cols(1, 0, 8)

    def cols_last():
        for g in range(2, 4):
            finish_rest(acc_j, (4 * g, min(4, NSYM - 4 * g)), NSYM + g, oj)
        return_cols(1, 8, NSYM - 8)

    arrive_col((0, 1), (1, 1), (-1, 1), (2, 1))
    arrive_row(1)
    arrive_row(7)
    arrive_col((0, 2), (1, 2), (-1, 2), (2, 2))
    arrive_row(2)
    arrive_row(6)
    arrive_col((0, 3), (1, 3), (-1, 3), (2, 3))
    arrive_row(3)
    arrive_row(5)
    arrive_col((1, 0))
    rows_ready(0, 1)
    prepare_rows(0)
    prepare_cols(0, 4, 0)
    rows_ready(7, 2)
    prepare_rows(1)

    def at_1():
        arrive_col((0, 4), (-1, 4), (2, 4))
        arrive_row(4)
        rows_ready(6, 3)
        prepare_rows(2)

    def at_2():
        for o in SYM[4:8]:
            arrive_col(o)
        prepare_cols(4, 4, 4)

    def at_5():
        for o in SYM[8:12]:
            arrive_col(o)
        prepare_cols(8, 4, 8)

    def at_8():
        rows_ready(5, 4)
        prepare_rows(3)

    def at_11():
        for g in range(4):
            prepare_rest(R, (4 * g, 4), NROW + g, True, B, vi)

    def at_14():
        arrive_col((2, 3))
        arrive_col((-1, 4))
        prepare_cols(12, 2, 12)
        for g in range(2):
            prepare_rest(C, (4 * g, 4), NSYM + g, False, A, vj)

    def at_19():
        arrive_col((2, 0))
        for g in range(2, 4):
            prepare_rest(C, (4 * g, min(4, NSYM - 4 * g)), NSYM + g, False, A, vj)
        prepare_cols(NSYM, 2, CHUNK_S)

    def at_20():
        arrive_col((2, 4))
        prepare_cols(NSYM + 2, 2, CHUNK_S + 2)
        prepare_rest(C, (NSYM, 4), CHUNK_S + 4, False, A, vj)

    actions = {
        1: at_1, 2: at_2, 5: at_5, 8: at_8, 11: at_11, 14: at_14, 16: cols_main, 19: at_19, 20: at_20, 21: cols_next,
        25: lambda: return_rows(3),
        27: lambda: return_rows(2),
        29: lambda: return_rows(1),
        STEPS: cols_last,
    }
    products(A, vj, B, vi, acc_i, acc_j, (d0, d1, d2, d3), (k0, k1, k2, k3), actions)
    return_rows(0)

    total = oi[0]
    for k, o in enumerate(SYM):
        backs[(*o, 0)].wait_recv()
        backs[(*o, 1)].wait_recv()
        total = total + gj[k]
    for dz in (*ROWS[:0:-1], 0):
        for dc in range(2):
            if (dz, dc) != (0, 0):
                backs[dz, dc].wait_recv()
                total = total + gi[rslot[(8 - dz) % 8] + dc]
    out_ref[:, 0:128] = total[0:32]
    rem = total[32:40]
    for q in range(4):
        turned = pltpu.roll(rem, (-32 * q) % 128, 1) if q else rem
        out_ref[8 * q : 8 * q + 8, 128:160] = turned[:, 0:32]
    for t in (*row.values(), *col.values(), *backs.values()):
        t.wait_send()


def per_device(points, vectors, lengthscales):
    vmem = pl.BlockSpec(memory_space=pltpu.VMEM)
    dma = pltpu.SemaphoreType.DMA
    return pl.pallas_call(
        solve_kernel,
        out_shape=jax.ShapeDtypeStruct(vectors.shape, F),
        in_specs=[pl.BlockSpec(memory_space=pl.ANY)] * 2 + [pl.BlockSpec(memory_space=pltpu.SMEM)],
        out_specs=vmem,
        scratch_shapes=[
            pltpu.VMEM(points.shape, F),
            pltpu.VMEM(vectors.shape, F),
            pltpu.VMEM((NROW, 64, 128), F),
            pltpu.VMEM((NCOL, 64, 128), F),
            pltpu.VMEM((128, NI), H),
            pltpu.VMEM((64, NI), H),
            pltpu.VMEM((NJ, 128), H),
            pltpu.VMEM((64, NJ), H),
            pltpu.VMEM((64, NI), F),
            pltpu.VMEM((64, NJ), F),
            *[pltpu.VMEM((TILE, TILE), F)] * 4,
            *[pltpu.VMEM((2, TILE, TILE), H)] * 4,
            pltpu.VMEM((NROW, 40, 128), F),
            pltpu.VMEM((NSYM, 40, 128), F),
            pltpu.VMEM((NROW, 40, 128), F),
            pltpu.VMEM((NSYM, 40, 128), F),
            dma((2,)),
            dma((NROW,)), dma((NROW,)), dma((NCOL,)), dma((NCOL,)),
            dma((NROW,)), dma((NROW,)), dma((2 * NSYM,)), dma((2 * NSYM,)),
        ],
        compiler_params=pltpu.CompilerParams(collective_id=0, has_side_effects=True),
        name="solve",
    )(points, vectors, lengthscales)


def solution(mesh):
    return jax.shard_map(
        per_device,
        mesh=mesh,
        in_specs=(P(None, ("blk", "rep")), P(None, ("blk", "rep")), P()),
        out_specs=P(None, ("blk", "rep")),
        check_vma=False,
    )
```

```python
import functools
import math
import jax
import jax.numpy as jnp
from jax import lax
from jax.experimental import pallas as pl
from jax.experimental.pallas import tpu as pltpu
from jax.sharding import PartitionSpec as P

F = jnp.float32
H = jnp.bfloat16
LN2 = math.log(2.0)
ALPHA = 1.5 / LN2
BETA = 0.75 / (LN2 * LN2)
SCALE = math.sqrt(5.0) / LN2
GAIN = (LN2 * LN2 / 3.0) * 2.0**ALPHA
TINY = 1e-30
TILE = 256

ROWS = [0, 1, 7, 2, 6, 3, 5, 4]
SYM = [(0, 1), (1, 0), (0, 2), (0, 3), (1, 1), (-1, 1), (1, 2), (-1, 2), (2, 1), (2, 2), (1, 3), (-1, 3), (2, 3), (-1, 4)]
OWN = [(0, 0), (2, 0), (0, 4), (2, 4)]
COLS = SYM + OWN
NROW, NCOL, NSYM = 16, len(COLS), len(SYM)
CHUNK_S = NSYM + -(-NSYM // 4)
NI, NJ = 128 * (NROW + NROW // 4), 128 * 24


def split3(value):
    first = value.astype(H).astype(F)
    rest = value - first
    second = rest.astype(H).astype(F)
    return first, second, rest - second


def stacked(*rows):
    index = lax.broadcasted_iota(jnp.int32, (16, 128), 0)
    out = jnp.zeros((16, 128), F)
    for k, value in enumerate(rows):
        out = jnp.where(index == k, value, out)
    return out


def pieces(z, row_side):
    square = jnp.sum(z * z, axis=0, keepdims=True)
    n1, n2, n3 = split3(square)
    x1, x2, x3 = split3(z)
    one, zero = jnp.ones_like(square), jnp.zeros((16, 128), F)
    if row_side:
        parts = [x1, x2, x1, x2, x3, x1, stacked(n1, n2, n3, one, one, one), zero]
    else:
        x1, x2, x3 = -2.0 * x1, -2.0 * x2, -2.0 * x3
        parts = [x1, x1, x2, x2, x1, x3, stacked(one, one, one, n1, n2, n3), zero]
    return jnp.concatenate(parts, axis=0)


def lanes(chunk):
    if isinstance(chunk, int):
        return pl.ds(128 * chunk, 128)
    return pl.ds(pl.multiple_of(chunk * 128, 128), 128)


def put(chunk, z, v, row_side, pts, vec):
    wide = pieces(z, row_side)
    if row_side:
        pts[:, lanes(chunk)] = wide.astype(H)
    else:
        pts[lanes(chunk), :] = wide.T.astype(H)
    high = v.astype(H)
    vec[0:32, lanes(chunk)] = high
    vec[32:64, lanes(chunk)] = (v - high.astype(F)).astype(H)


def prepare(src, slots, chunk0, row_side, pts, vec):
    first, count = slots

    @pl.loop(0, count)
    def _(s):
        put(chunk0 + s, src[first + s, 0:16, :], src[first + s, 16:48, :], row_side, pts, vec)


def prepare_rest(src, slots, chunk, row_side, pts, vec):
    first, count = slots
    group_of = lax.broadcasted_iota(jnp.int32, (16, 128), 1) // 32
    outs = [jnp.zeros((16, 128), F) for _ in range(3)]
    for k in range(count):
        rem = src[first + k, 48:64, :]
        for q in range(3):
            turn = (32 * (k - q)) % 128
            outs[q] = jnp.where(group_of == k, pltpu.roll(rem, turn, 1) if turn else rem, outs[q])
    put(chunk, outs[0], jnp.concatenate(outs[1:], axis=0), row_side, pts, vec)


def finish_main(acc, slots, chunk0, out):
    first, count = slots
    for k in range(count):
        c = lanes(chunk0 + k)
        out[first + k, 0:32, :] = (acc[0:32, c] + acc[32:64, c]) * GAIN


def finish_rest(acc, slots, rest, out):
    first, count = slots
    group_of = lax.broadcasted_iota(jnp.int32, (8, 128), 1) // 32
    c = lanes(rest)
    t = (acc[0:32, c] + acc[32:64, c]) * GAIN
    for k in range(count):
        o = jnp.zeros((8, 128), F)
        for q in range(4):
            turn = (32 * (q - k)) % 128
            piece = t[8 * q : 8 * q + 8, :]
            o = jnp.where(group_of == q, pltpu.roll(piece, turn, 1) if turn else piece, o)
        out[first + k, 32:40, :] = o


def block_of(m):
    def pick(cond, yes, no):
        return jnp.where(cond, yes, no)

    third = pick(m >= 6, 2, pick(m >= 3, 1, 0))
    tail = m - 15
    fifth = pick(m >= 27, 4, pick(m >= 24, 3, pick(m >= 21, 2, pick(m >= 18, 1, 0))))
    j = pick(m < 9, third, pick(m < 12, m - 9, pick(m < 15, m - 12, 3 + tail - 3 * fifth)))
    i = pick(m < 9, m - 3 * third, pick(m < 12, 3, pick(m < 15, 4, 4 - fifth)))
    return j, i


STEPS = 30


def products(A, vj, B, vi, acc_i, acc_j, d, k, actions):
    def place(block, q):
        j, i = block
        return (
            pl.ds(pl.multiple_of((2 * j + q // 2) * TILE, TILE), TILE),
            pl.ds(pl.multiple_of((2 * i + q % 2) * TILE, TILE), TILE),
        )

    def distances(block, q):
        sj, si = place(block, q)
        d[q][...] = jnp.dot(A[sj, :], B[:, si], preferred_element_type=F)

    def kernel_values(q):
        x = jnp.maximum(d[q][...], TINY)
        u = (-ALPHA) - x * lax.rsqrt(x)
        value = (u * u + BETA) * jnp.exp2(u)
        high = value.astype(H)
        k[q][0] = high
        k[q][1] = (value - high.astype(F)).astype(H)

    def accumulate(block, q):
        sj, si = place(block, q)
        v_j, v_i = vj[:, sj], vi[:, si]
        acc_i[:, si] += jnp.dot(
            jnp.concatenate([v_j, v_j], axis=1), jnp.concatenate([k[q][0], k[q][1]], axis=0), preferred_element_type=F
        )
        acc_j[:, sj] += jnp.dot(
            jnp.concatenate([v_i, v_i], axis=1), jnp.concatenate([k[q][0].T, k[q][1].T], axis=0), preferred_element_type=F
        )

    for q in range(3):
        distances(block_of(jnp.int32(0)), q)
    for q in range(1, 4):
        k[q][...] = jnp.zeros_like(k[q])

    def step(m, blocks):
        for at, action in actions.items():
            if at < STEPS:
                pl.when(m == at)(action)
        before, now, after = blocks
        for q in range(4):
            distances(after if q else now, (q + 3) % 4)
            accumulate(before if q < 3 else now, (q + 1) % 4)
            kernel_values(q)
        return now, after, block_of(jnp.minimum(m + 2, STEPS - 1))

    start = block_of(jnp.int32(0))
    lax.fori_loop(0, STEPS, step, (start, start, block_of(jnp.int32(1))))
    actions[STEPS]()
    for q in range(1, 4):
        accumulate(block_of(jnp.int32(STEPS - 1)), q)


def solve_kernel(p_hbm, v_hbm, l_ref, out_ref, p_ref, v_ref, R, C, B, vi, A, vj, acc_i, acc_j, d0, d1, d2, d3, k0, k1, k2, k3,
                 oi, oj, gi, gj, io, rs, rr, cs, cr, ris, rir, cjs, cjr):
    b, r = lax.axis_index("blk"), lax.axis_index("rep")
    core, z, x = lax.rem(b, 2), lax.div(b, 8), lax.rem(r, 4)
    y = lax.div(r, 4) * 4 + lax.rem(lax.div(b, 2), 4)

    def at(dx=0, dy=0, dz=0, dc=0):
        xx, yy, zz = lax.rem(x + dx + 4, 4), lax.rem(y + dy + 8, 8), lax.rem(z + dz + 8, 8)
        cc = 1 - core if dc else core
        return ((zz * 4 + lax.rem(yy, 4)) * 2 + cc, lax.div(yy, 4) * 4 + xx)

    barrier = pltpu.get_barrier_semaphore()
    near = [at(dc=1)] + [at(dz=k) for k in range(1, 8)] + [at(dy=k) for k in range(1, 8)] + [at(dx=k) for k in range(1, 4)]
    for d in near:
        pl.semaphore_signal(barrier, inc=1, device_id=d, device_id_type=pl.DeviceIdType.MESH)
    loads = [pltpu.make_async_copy(p_hbm, p_ref, io.at[0]), pltpu.make_async_copy(v_hbm, v_ref, io.at[1])]
    for t in loads:
        t.start()
    feature = lax.broadcasted_iota(jnp.int32, (16, 160), 0)
    scale = jnp.ones((16, 160), F)
    for f in range(16):
        scale = jnp.where(feature == f, l_ref[f], scale)
    acc_i[...] = jnp.zeros_like(acc_i)
    acc_j[...] = jnp.zeros_like(acc_j)
    pad = pl.ds(NJ - 128, 128)
    A[pad, :] = jnp.zeros((128, 128), H)
    vj[:, pad] = jnp.zeros((64, 128), H)
    for t in loads:
        t.wait()

    own = R.at[0]
    scaled = p_ref[...] / scale * SCALE
    R[0, 0:16, :] = scaled[:, 0:128]
    R[0, 16:48, :] = v_ref[:, 0:128]
    R[0, 48:64, 0:32] = scaled[:, 128:160]
    R[0, 48:64, 32:64] = v_ref[0:16, 128:160]
    R[0, 48:64, 64:96] = v_ref[16:32, 128:160]
    R[0, 48:64, 96:128] = jnp.zeros((16, 32), F)
    C[NSYM] = R[0]
    pl.semaphore_wait(barrier, len(near))

    def send(source, dest, ss, rsem, where):
        return pltpu.make_async_remote_copy(
            src_ref=source, dst_ref=dest, send_sem=ss, recv_sem=rsem, device_id=where,
            device_id_type=pl.DeviceIdType.MESH,
        )

    row, col = {}, {}
    rslot = {dz: 2 * k for k, dz in enumerate(ROWS)}
    for dz in range(8):
        for dc in range(2):
            s = rslot[dz] + dc
            if s == 0:
                continue
            if dc:
                source, where = R.at[rslot[dz]], at(dc=1)
            else:
                source, where = own, at(dz=-dz)
            row[dz, dc] = send(source, R.at[s], rs.at[s], rr.at[s], where)
    slot = {o: k for k, o in enumerate(COLS)}
    for (dx, dy), s in slot.items():
        if (dx, dy) == (0, 0):
            continue
        if dx == 0:
            prev, where = (0, 0), at(dy=-dy)
        else:
            prev, where = (0, dy), at(dx=-dx)
        source = own if prev == (0, 0) else C.at[slot[prev]]
        col[dx, dy] = send(source, C.at[s], cs.at[s], cr.at[s], where)

    for t in (col[0, 1], row[1, 0], row[7, 0], col[1, 0], row[0, 1], col[0, 2], row[2, 0], row[6, 0], col[2, 0],
              col[0, 3], row[3, 0], row[5, 0], col[0, 4], row[4, 0]):
        t.start()

    def arrive_row(dz, *then):
        row[dz, 0].wait_recv()
        for t in then:
            row[t, 0].start()
        row[dz, 1].start()

    def arrive_col(o, *then):
        col[o].wait_recv()
        for t in then:
            col[t].start()

    def rows_ready(*offsets):
        for dz in offsets:
            row[dz, 1].wait_recv()

    def prepare_rows(group):
        prepare(R, (4 * group, 4), 4 * group, True, B, vi)

    def prepare_cols(first, count, chunk):
        prepare(C, (first, count), chunk, False, A, vj)

    backs = {}

    def back(key, source, dest, ss, rsem, where):
        backs[key] = send(source, dest, ss, rsem, where)

    for k, (dx, dy) in enumerate(SYM):
        for part, rows in enumerate((pl.ds(0, 32), pl.ds(32, 8))):
            e = 2 * k + part
            back((dx, dy, part), oj.at[k, rows], gj.at[k, rows], cjs.at[e], cjr.at[e], at(dx=dx, dy=dy))
    for dz in range(8):
        for dc in range(2):
            if (dz, dc) != (0, 0):
                s, d = rslot[dz] + dc, rslot[(8 - dz) % 8] + dc
                back((dz, dc), oi.at[s], gi.at[d], ris.at[d], rir.at[d], at(dz=dz, dc=dc))

    def return_rows(group):
        finish_main(acc_i, (4 * group, 4), 4 * group, oi)
        finish_rest(acc_i, (4 * group, 4), NROW + group, oi)
        for k in (2 * group + 1, 2 * group):
            for dc in range(2):
                if (ROWS[k], dc) != (0, 0):
                    backs[ROWS[k], dc].start()

    def return_cols(part, first, count):
        for o in SYM[first : first + count]:
            backs[(*o, part)].start()

    def cols_main():
        finish_main(acc_j, (0, 12), 0, oj)
        return_cols(0, 0, 12)

    def at_16():
        own_rest()
        cols_main()

    def cols_next():
        finish_main(acc_j, (12, 2), 12, oj)
        for g in range(2):
            finish_rest(acc_j, (4 * g, 4), NSYM + g, oj)
        return_cols(0, 12, 2)
        return_cols(1, 0, 8)

    def cols_last():
        for g in range(2, 4):
            finish_rest(acc_j, (4 * g, min(4, NSYM - 4 * g)), NSYM + g, oj)
        return_cols(1, 8, NSYM - 8)

    arrive_col((0, 1), (1, 1), (-1, 1), (2, 1))
    arrive_row(1)
    arrive_row(7)
    arrive_col((0, 2), (1, 2), (-1, 2), (2, 2))
    arrive_row(2)
    arrive_row(6)
    arrive_col((0, 3), (1, 3), (-1, 3), (2, 3))
    arrive_row(3)
    arrive_row(5)
    arrive_col((1, 0))
    rows_ready(0, 1)
    prepare_rows(0)
    prepare_cols(0, 4, 0)
    rows_ready(7, 2)
    prepare_rows(1)

    def at_1():
        arrive_col((0, 4), (-1, 4), (2, 4))
        arrive_row(4)
        rows_ready(6, 3)
        prepare_rows(2)

    def at_2():
        for o in SYM[4:8]:
            arrive_col(o)
        prepare_cols(4, 4, 4)

    def at_5():
        for o in SYM[8:12]:
            arrive_col(o)
        prepare_cols(8, 4, 8)

    def at_8():
        rows_ready(5, 4)
        prepare_rows(3)

    def at_11():
        for g in range(4):
            prepare_rest(R, (4 * g, 4), NROW + g, True, B, vi)

    def at_14():
        arrive_col((2, 3))
        arrive_col((-1, 4))
        prepare_cols(12, 2, 12)
        for g in range(2):
            prepare_rest(C, (4 * g, 4), NSYM + g, False, A, vj)

    def at_15():
        arrive_col((2, 0))
        for g in range(2, 4):
            prepare_rest(C, (4 * g, min(4, NSYM - 4 * g)), NSYM + g, False, A, vj)
        prepare_cols(NSYM, 2, CHUNK_S)

    def own_rest():
        arrive_col((2, 4))
        prepare_cols(NSYM + 2, 2, CHUNK_S + 2)
        prepare_rest(C, (NSYM, 4), CHUNK_S + 4, False, A, vj)

    actions = {
        1: at_1, 2: at_2, 5: at_5, 8: at_8, 11: at_11, 14: at_14, 15: at_15, 16: at_16,
        22: lambda: return_rows(3),
        25: lambda: return_rows(2),
        28: lambda: return_rows(1),
        29: cols_next,
        STEPS: cols_last,
    }
    products(A, vj, B, vi, acc_i, acc_j, (d0, d1, d2, d3), (k0, k1, k2, k3), actions)
    return_rows(0)

    total = oi[0]
    for k, o in enumerate(SYM):
        backs[(*o, 0)].wait_recv()
        backs[(*o, 1)].wait_recv()
        total = total + gj[k]
    for dz in (*ROWS[:0:-1], 0):
        for dc in range(2):
            if (dz, dc) != (0, 0):
                backs[dz, dc].wait_recv()
                total = total + gi[rslot[(8 - dz) % 8] + dc]
    out_ref[:, 0:128] = total[0:32]
    rem = total[32:40]
    for q in range(4):
        turned = pltpu.roll(rem, (-32 * q) % 128, 1) if q else rem
        out_ref[8 * q : 8 * q + 8, 128:160] = turned[:, 0:32]
    for t in (*row.values(), *col.values(), *backs.values()):
        t.wait_send()


def per_device(points, vectors, lengthscales):
    vmem = pl.BlockSpec(memory_space=pltpu.VMEM)
    dma = pltpu.SemaphoreType.DMA
    return pl.pallas_call(
        solve_kernel,
        out_shape=jax.ShapeDtypeStruct(vectors.shape, F),
        in_specs=[pl.BlockSpec(memory_space=pl.ANY)] * 2 + [pl.BlockSpec(memory_space=pltpu.SMEM)],
        out_specs=vmem,
        scratch_shapes=[
            pltpu.VMEM(points.shape, F),
            pltpu.VMEM(vectors.shape, F),
            pltpu.VMEM((NROW, 64, 128), F),
            pltpu.VMEM((NCOL, 64, 128), F),
            pltpu.VMEM((128, NI), H),
            pltpu.VMEM((64, NI), H),
            pltpu.VMEM((NJ, 128), H),
            pltpu.VMEM((64, NJ), H),
            pltpu.VMEM((64, NI), F),
            pltpu.VMEM((64, NJ), F),
            *[pltpu.VMEM((TILE, TILE), F)] * 4,
            *[pltpu.VMEM((2, TILE, TILE), H)] * 4,
            pltpu.VMEM((NROW, 40, 128), F),
            pltpu.VMEM((NSYM, 40, 128), F),
            pltpu.VMEM((NROW, 40, 128), F),
            pltpu.VMEM((NSYM, 40, 128), F),
            dma((2,)),
            dma((NROW,)), dma((NROW,)), dma((NCOL,)), dma((NCOL,)),
            dma((NROW,)), dma((NROW,)), dma((2 * NSYM,)), dma((2 * NSYM,)),
        ],
        compiler_params=pltpu.CompilerParams(collective_id=0, has_side_effects=True),
        name="solve",
    )(points, vectors, lengthscales)


def solution(mesh):
    return jax.shard_map(
        per_device,
        mesh=mesh,
        in_specs=(P(None, ("blk", "rep")), P(None, ("blk", "rep")), P()),
        out_specs=P(None, ("blk", "rep")),
        check_vma=False,
    )
```

```python
import functools
import math
import jax
import jax.numpy as jnp
from jax import lax
from jax.experimental import pallas as pl
from jax.experimental.pallas import tpu as pltpu
from jax.sharding import PartitionSpec as P

F = jnp.float32
H = jnp.bfloat16
LN2 = math.log(2.0)
ALPHA = 1.5 / LN2
BETA = 0.75 / (LN2 * LN2)
SCALE = math.sqrt(5.0) / LN2
GAIN = (LN2 * LN2 / 3.0) * 2.0**ALPHA
TINY = 1e-30
TILE = 256

ROWS = [0, 1, 7, 2, 6, 3, 5, 4]
SYM = [(0, 1), (1, 0), (0, 2), (0, 3), (1, 1), (-1, 1), (1, 2), (-1, 2), (2, 1), (2, 2), (1, 3), (-1, 3), (2, 3), (-1, 4)]
OWN = [(0, 0), (2, 0), (0, 4), (2, 4)]
COLS = SYM + OWN
NROW, NCOL, NSYM = 16, len(COLS), len(SYM)
CHUNK_S = NSYM + -(-NSYM // 4)
REST = [(6, 4), (10, 4), (0, 4), (4, 2)]
NI, NJ = 128 * (NROW + NROW // 4), 128 * 24


def split3(value):
    first = value.astype(H).astype(F)
    rest = value - first
    second = rest.astype(H).astype(F)
    return first, second, rest - second


def stacked(*rows):
    index = lax.broadcasted_iota(jnp.int32, (16, 128), 0)
    out = jnp.zeros((16, 128), F)
    for k, value in enumerate(rows):
        out = jnp.where(index == k, value, out)
    return out


def pieces(z, row_side):
    square = jnp.sum(z * z, axis=0, keepdims=True)
    n1, n2, n3 = split3(square)
    x1, x2, x3 = split3(z)
    one, zero = jnp.ones_like(square), jnp.zeros((16, 128), F)
    if row_side:
        parts = [x1, x2, x1, x2, x3, x1, stacked(n1, n2, n3, one, one, one), zero]
    else:
        x1, x2, x3 = -2.0 * x1, -2.0 * x2, -2.0 * x3
        parts = [x1, x1, x2, x2, x1, x3, stacked(one, one, one, n1, n2, n3), zero]
    return jnp.concatenate(parts, axis=0)


def lanes(chunk):
    if isinstance(chunk, int):
        return pl.ds(128 * chunk, 128)
    return pl.ds(pl.multiple_of(chunk * 128, 128), 128)


def put(chunk, z, v, row_side, pts, vec):
    wide = pieces(z, row_side)
    if row_side:
        pts[:, lanes(chunk)] = wide.astype(H)
    else:
        pts[lanes(chunk), :] = wide.T.astype(H)
    high = v.astype(H)
    vec[0:32, lanes(chunk)] = high
    vec[32:64, lanes(chunk)] = (v - high.astype(F)).astype(H)


def prepare(src, slots, chunk0, row_side, pts, vec):
    first, count = slots

    @pl.loop(0, count)
    def _(s):
        put(chunk0 + s, src[first + s, 0:16, :], src[first + s, 16:48, :], row_side, pts, vec)


def prepare_rest(src, slots, chunk, row_side, pts, vec):
    first, count = slots
    group_of = lax.broadcasted_iota(jnp.int32, (16, 128), 1) // 32
    outs = [jnp.zeros((16, 128), F) for _ in range(3)]
    for k in range(count):
        rem = src[first + k, 48:64, :]
        for q in range(3):
            turn = (32 * (k - q)) % 128
            outs[q] = jnp.where(group_of == k, pltpu.roll(rem, turn, 1) if turn else rem, outs[q])
    put(chunk, outs[0], jnp.concatenate(outs[1:], axis=0), row_side, pts, vec)


def finish_main(acc, slots, chunk0, out):
    first, count = slots
    for k in range(count):
        c = lanes(chunk0 + k)
        out[first + k, 0:32, :] = (acc[0:32, c] + acc[32:64, c]) * GAIN


def finish_rest(acc, slots, rest, out):
    first, count = slots
    group_of = lax.broadcasted_iota(jnp.int32, (8, 128), 1) // 32
    c = lanes(rest)
    t = (acc[0:32, c] + acc[32:64, c]) * GAIN
    for k in range(count):
        o = jnp.zeros((8, 128), F)
        for q in range(4):
            turn = (32 * (q - k)) % 128
            piece = t[8 * q : 8 * q + 8, :]
            o = jnp.where(group_of == q, pltpu.roll(piece, turn, 1) if turn else piece, o)
        out[first + k, 32:40, :] = o


def block_of(m):
    def pick(cond, yes, no):
        return jnp.where(cond, yes, no)

    third = pick(m >= 6, 2, pick(m >= 3, 1, 0))
    pair = lax.shift_right_logical(jnp.maximum(m - 20, 0), 1)
    j = pick(m < 9, third, pick(m < 12, m - 9, pick(m < 15, m - 12, pick(m < 20, 3, m - 16 - 2 * pair))))
    i = pick(m < 9, m - 3 * third, pick(m < 12, 3, pick(m < 15, 4, pick(m < 20, m - 15, 4 - pair))))
    return j, i


STEPS = 30


def products(A, vj, B, vi, acc_i, acc_j, d, k, actions):
    def place(block, q):
        j, i = block
        return (
            pl.ds(pl.multiple_of((2 * j + q // 2) * TILE, TILE), TILE),
            pl.ds(pl.multiple_of((2 * i + q % 2) * TILE, TILE), TILE),
        )

    def distances(block, q):
        sj, si = place(block, q)
        d[q][...] = jnp.dot(A[sj, :], B[:, si], preferred_element_type=F)

    def kernel_values(q):
        x = jnp.maximum(d[q][...], TINY)
        u = (-ALPHA) - x * lax.rsqrt(x)
        value = (u * u + BETA) * jnp.exp2(u)
        high = value.astype(H)
        k[q][0] = high
        k[q][1] = (value - high.astype(F)).astype(H)

    def accumulate(block, q):
        sj, si = place(block, q)
        v_j, v_i = vj[:, sj], vi[:, si]
        acc_i[:, si] += jnp.dot(
            jnp.concatenate([v_j, v_j], axis=1), jnp.concatenate([k[q][0], k[q][1]], axis=0), preferred_element_type=F
        )
        acc_j[:, sj] += jnp.dot(
            jnp.concatenate([v_i, v_i], axis=1), jnp.concatenate([k[q][0].T, k[q][1].T], axis=0), preferred_element_type=F
        )

    for q in range(3):
        distances(block_of(jnp.int32(0)), q)
    for q in range(1, 4):
        k[q][...] = jnp.zeros_like(k[q])

    def step(m, blocks):
        for at, action in actions.items():
            if at < STEPS:
                pl.when(m == at)(action)
        before, now, after = blocks
        for q in range(4):
            distances(after if q else now, (q + 3) % 4)
            accumulate(before if q < 3 else now, (q + 1) % 4)
            kernel_values(q)
        return now, after, block_of(jnp.minimum(m + 2, STEPS - 1))

    start = block_of(jnp.int32(0))
    lax.fori_loop(0, STEPS, step, (start, start, block_of(jnp.int32(1))))
    actions[STEPS]()
    for q in range(1, 4):
        accumulate(block_of(jnp.int32(STEPS - 1)), q)


def solve_kernel(p_hbm, v_hbm, l_ref, out_ref, p_ref, v_ref, R, C, B, vi, A, vj, acc_i, acc_j, d0, d1, d2, d3, k0, k1, k2, k3,
                 oi, oj, gi, gj, io, rs, rr, cs, cr, ris, rir, cjs, cjr):
    b, r = lax.axis_index("blk"), lax.axis_index("rep")
    core, z, x = lax.rem(b, 2), lax.div(b, 8), lax.rem(r, 4)
    y = lax.div(r, 4) * 4 + lax.rem(lax.div(b, 2), 4)

    def at(dx=0, dy=0, dz=0, dc=0):
        xx, yy, zz = lax.rem(x + dx + 4, 4), lax.rem(y + dy + 8, 8), lax.rem(z + dz + 8, 8)
        cc = 1 - core if dc else core
        return ((zz * 4 + lax.rem(yy, 4)) * 2 + cc, lax.div(yy, 4) * 4 + xx)

    barrier = pltpu.get_barrier_semaphore()
    near = [at(dc=1)] + [at(dz=k) for k in range(1, 8)] + [at(dy=k) for k in range(1, 8)] + [at(dx=k) for k in range(1, 4)]
    for d in near:
        pl.semaphore_signal(barrier, inc=1, device_id=d, device_id_type=pl.DeviceIdType.MESH)
    loads = [pltpu.make_async_copy(p_hbm, p_ref, io.at[0]), pltpu.make_async_copy(v_hbm, v_ref, io.at[1])]
    for t in loads:
        t.start()
    feature = lax.broadcasted_iota(jnp.int32, (16, 160), 0)
    scale = jnp.ones((16, 160), F)
    for f in range(16):
        scale = jnp.where(feature == f, l_ref[f], scale)
    acc_i[...] = jnp.zeros_like(acc_i)
    acc_j[...] = jnp.zeros_like(acc_j)
    pad = pl.ds(NJ - 128, 128)
    A[pad, :] = jnp.zeros((128, 128), H)
    vj[:, pad] = jnp.zeros((64, 128), H)
    for t in loads:
        t.wait()

    own = R.at[0]
    scaled = p_ref[...] / scale * SCALE
    R[0, 0:16, :] = scaled[:, 0:128]
    R[0, 16:48, :] = v_ref[:, 0:128]
    R[0, 48:64, 0:32] = scaled[:, 128:160]
    R[0, 48:64, 32:64] = v_ref[0:16, 128:160]
    R[0, 48:64, 64:96] = v_ref[16:32, 128:160]
    R[0, 48:64, 96:128] = jnp.zeros((16, 32), F)
    C[NSYM] = R[0]
    pl.semaphore_wait(barrier, len(near))

    def send(source, dest, ss, rsem, where):
        return pltpu.make_async_remote_copy(
            src_ref=source, dst_ref=dest, send_sem=ss, recv_sem=rsem, device_id=where,
            device_id_type=pl.DeviceIdType.MESH,
        )

    row, col = {}, {}
    rslot = {dz: 2 * k for k, dz in enumerate(ROWS)}
    for dz in range(8):
        for dc in range(2):
            s = rslot[dz] + dc
            if s == 0:
                continue
            if dc:
                source, where = R.at[rslot[dz]], at(dc=1)
            else:
                source, where = own, at(dz=-dz)
            row[dz, dc] = send(source, R.at[s], rs.at[s], rr.at[s], where)
    slot = {o: k for k, o in enumerate(COLS)}
    for (dx, dy), s in slot.items():
        if (dx, dy) == (0, 0):
            continue
        if dx == 0:
            prev, where = (0, 0), at(dy=-dy)
        else:
            prev, where = (0, dy), at(dx=-dx)
        source = own if prev == (0, 0) else C.at[slot[prev]]
        col[dx, dy] = send(source, C.at[s], cs.at[s], cr.at[s], where)

    for t in (col[0, 1], row[1, 0], row[7, 0], col[1, 0], row[0, 1], col[0, 2], row[2, 0], row[6, 0], col[2, 0],
              col[0, 3], row[3, 0], row[5, 0], col[0, 4], row[4, 0]):
        t.start()

    def arrive_row(dz, *then):
        row[dz, 0].wait_recv()
        for t in then:
            row[t, 0].start()
        row[dz, 1].start()

    def arrive_col(o, *then):
        col[o].wait_recv()
        for t in then:
            col[t].start()

    def rows_ready(*offsets):
        for dz in offsets:
            row[dz, 1].wait_recv()

    def prepare_rows(group):
        prepare(R, (4 * group, 4), 4 * group, True, B, vi)

    def prepare_cols(first, count, chunk):
        prepare(C, (first, count), chunk, False, A, vj)

    backs = {}

    def back(key, source, dest, ss, rsem, where):
        backs[key] = send(source, dest, ss, rsem, where)

    for k, (dx, dy) in enumerate(SYM):
        for part, rows in enumerate((pl.ds(0, 32), pl.ds(32, 8))):
            e = 2 * k + part
            back((dx, dy, part), oj.at[k, rows], gj.at[k, rows], cjs.at[e], cjr.at[e], at(dx=dx, dy=dy))
    for dz in range(8):
        for dc in range(2):
            if (dz, dc) != (0, 0):
                s, d = rslot[dz] + dc, rslot[(8 - dz) % 8] + dc
                back((dz, dc), oi.at[s], gi.at[d], ris.at[d], rir.at[d], at(dz=dz, dc=dc))

    def return_rows(group):
        finish_main(acc_i, (4 * group, 4), 4 * group, oi)
        finish_rest(acc_i, (4 * group, 4), NROW + group, oi)
        for k in (2 * group + 1, 2 * group):
            for dc in range(2):
                if (ROWS[k], dc) != (0, 0):
                    backs[ROWS[k], dc].start()

    def return_cols(part, first, count):
        for o in SYM[first : first + count]:
            backs[(*o, part)].start()

    def cols_main():
        finish_main(acc_j, (0, 12), 0, oj)
        return_cols(0, 0, 12)

    def cols_next():
        finish_main(acc_j, (12, 2), 12, oj)
        for g in range(2):
            finish_rest(acc_j, REST[g], NSYM + g, oj)
        return_cols(0, 12, 2)
        return_cols(1, 6, 8)

    def cols_last():
        for g in range(2, 4):
            finish_rest(acc_j, REST[g], NSYM + g, oj)
        return_cols(1, 0, 6)

    arrive_col((0, 1), (1, 1), (-1, 1), (2, 1))
    arrive_row(1)
    arrive_row(7)
    arrive_col((0, 2), (1, 2), (-1, 2), (2, 2))
    arrive_row(2)
    arrive_row(6)
    arrive_col((0, 3), (1, 3), (-1, 3), (2, 3))
    arrive_row(3)
    arrive_row(5)
    arrive_col((1, 0))
    rows_ready(0, 1)
    prepare_rows(0)
    prepare_cols(0, 4, 0)
    rows_ready(7, 2)
    prepare_rows(1)

    def at_1():
        arrive_col((0, 4), (-1, 4), (2, 4))
        arrive_row(4)
        rows_ready(6, 3)
        prepare_rows(2)

    def at_2():
        for o in SYM[4:8]:
            arrive_col(o)
        prepare_cols(4, 4, 4)

    def at_5():
        for o in SYM[8:12]:
            arrive_col(o)
        prepare_cols(8, 4, 8)

    def at_8():
        rows_ready(5, 4)
        prepare_rows(3)

    def at_11():
        for g in range(4):
            prepare_rest(R, (4 * g, 4), NROW + g, True, B, vi)

    def at_14():
        arrive_col((2, 3))
        arrive_col((-1, 4))
        prepare_cols(12, 2, 12)
        for g in range(2):
            prepare_rest(C, REST[g], NSYM + g, False, A, vj)

    def at_19():
        arrive_col((2, 0))
        for g in range(2, 4):
            prepare_rest(C, REST[g], NSYM + g, False, A, vj)
        prepare_cols(NSYM, 2, CHUNK_S)

    def at_20():
        arrive_col((2, 4))
        prepare_cols(NSYM + 2, 2, CHUNK_S + 2)
        prepare_rest(C, (NSYM, 4), CHUNK_S + 4, False, A, vj)

    actions = {
        1: at_1, 2: at_2, 5: at_5, 8: at_8, 11: at_11, 14: at_14, 16: cols_main, 19: at_19, 20: at_20, 21: cols_next,
        25: lambda: return_rows(3),
        27: lambda: return_rows(2),
        29: lambda: return_rows(1),
        STEPS: cols_last,
    }
    products(A, vj, B, vi, acc_i, acc_j, (d0, d1, d2, d3), (k0, k1, k2, k3), actions)
    return_rows(0)

    total = oi[0]
    for k, o in enumerate(SYM):
        backs[(*o, 0)].wait_recv()
        backs[(*o, 1)].wait_recv()
        total = total + gj[k]
    for dz in (*ROWS[:0:-1], 0):
        for dc in range(2):
            if (dz, dc) != (0, 0):
                backs[dz, dc].wait_recv()
                total = total + gi[rslot[(8 - dz) % 8] + dc]
    out_ref[:, 0:128] = total[0:32]
    rem = total[32:40]
    for q in range(4):
        turned = pltpu.roll(rem, (-32 * q) % 128, 1) if q else rem
        out_ref[8 * q : 8 * q + 8, 128:160] = turned[:, 0:32]
    for t in (*row.values(), *col.values(), *backs.values()):
        t.wait_send()


def per_device(points, vectors, lengthscales):
    vmem = pl.BlockSpec(memory_space=pltpu.VMEM)
    dma = pltpu.SemaphoreType.DMA
    return pl.pallas_call(
        solve_kernel,
        out_shape=jax.ShapeDtypeStruct(vectors.shape, F),
        in_specs=[pl.BlockSpec(memory_space=pl.ANY)] * 2 + [pl.BlockSpec(memory_space=pltpu.SMEM)],
        out_specs=vmem,
        scratch_shapes=[
            pltpu.VMEM(points.shape, F),
            pltpu.VMEM(vectors.shape, F),
            pltpu.VMEM((NROW, 64, 128), F),
            pltpu.VMEM((NCOL, 64, 128), F),
            pltpu.VMEM((128, NI), H),
            pltpu.VMEM((64, NI), H),
            pltpu.VMEM((NJ, 128), H),
            pltpu.VMEM((64, NJ), H),
            pltpu.VMEM((64, NI), F),
            pltpu.VMEM((64, NJ), F),
            *[pltpu.VMEM((TILE, TILE), F)] * 4,
            *[pltpu.VMEM((2, TILE, TILE), H)] * 4,
            pltpu.VMEM((NROW, 40, 128), F),
            pltpu.VMEM((NSYM, 40, 128), F),
            pltpu.VMEM((NROW, 40, 128), F),
            pltpu.VMEM((NSYM, 40, 128), F),
            dma((2,)),
            dma((NROW,)), dma((NROW,)), dma((NCOL,)), dma((NCOL,)),
            dma((NROW,)), dma((NROW,)), dma((2 * NSYM,)), dma((2 * NSYM,)),
        ],
        compiler_params=pltpu.CompilerParams(collective_id=0, has_side_effects=True),
        name="solve",
    )(points, vectors, lengthscales)


def solution(mesh):
    return jax.shard_map(
        per_device,
        mesh=mesh,
        in_specs=(P(None, ("blk", "rep")), P(None, ("blk", "rep")), P()),
        out_specs=P(None, ("blk", "rep")),
        check_vma=False,
    )
```

```python
import functools
import math
import jax
import jax.numpy as jnp
from jax import lax
from jax.experimental import pallas as pl
from jax.experimental.pallas import tpu as pltpu
from jax.sharding import PartitionSpec as P

F = jnp.float32
H = jnp.bfloat16
LN2 = math.log(2.0)
ALPHA = 1.5 / LN2
BETA = 0.75 / (LN2 * LN2)
SCALE = math.sqrt(5.0) / LN2
GAIN = (LN2 * LN2 / 3.0) * 2.0**ALPHA
TINY = 1e-30
TILE = 256

ROWS = [0, 1, 7, 2, 6, 3, 5, 4]
SYM = [(0, 1), (1, 0), (0, 2), (0, 3), (1, 1), (-1, 1), (1, 2), (-1, 2), (2, 1), (2, 2), (1, 3), (-1, 3), (2, 3), (-1, 4)]
OWN = [(0, 0), (2, 0), (0, 4), (2, 4)]
COLS = SYM + OWN
NROW, NCOL, NSYM = 16, len(COLS), len(SYM)
CHUNK_S = NSYM + -(-NSYM // 4)
REST = [(6, 4), (10, 4), (0, 4), (4, 2)]
NI, NJ = 128 * (NROW + NROW // 4), 128 * 24


def split3(value):
    first = value.astype(H).astype(F)
    rest = value - first
    second = rest.astype(H).astype(F)
    return first, second, rest - second


def stacked(*rows):
    index = lax.broadcasted_iota(jnp.int32, (16, 128), 0)
    out = jnp.zeros((16, 128), F)
    for k, value in enumerate(rows):
        out = jnp.where(index == k, value, out)
    return out


def pieces(z, row_side):
    square = jnp.sum(z * z, axis=0, keepdims=True)
    n1, n2, n3 = split3(square)
    x1, x2, x3 = split3(z)
    one, zero = jnp.ones_like(square), jnp.zeros((16, 128), F)
    if row_side:
        parts = [x1, x2, x1, x2, x3, x1, stacked(n1, n2, n3, one, one, one), zero]
    else:
        x1, x2, x3 = -2.0 * x1, -2.0 * x2, -2.0 * x3
        parts = [x1, x1, x2, x2, x1, x3, stacked(one, one, one, n1, n2, n3), zero]
    return jnp.concatenate(parts, axis=0)


def lanes(chunk):
    if isinstance(chunk, int):
        return pl.ds(128 * chunk, 128)
    return pl.ds(pl.multiple_of(chunk * 128, 128), 128)


def put(chunk, z, v, row_side, pts, vec):
    wide = pieces(z, row_side)
    if row_side:
        pts[:, lanes(chunk)] = wide.astype(H)
    else:
        pts[lanes(chunk), :] = wide.T.astype(H)
    high = v.astype(H)
    vec[0:32, lanes(chunk)] = high
    vec[32:64, lanes(chunk)] = (v - high.astype(F)).astype(H)


def prepare(src, slots, chunk0, row_side, pts, vec):
    first, count = slots

    @pl.loop(0, count)
    def _(s):
        put(chunk0 + s, src[first + s, 0:16, :], src[first + s, 16:48, :], row_side, pts, vec)


def prepare_rest(src, slots, chunk, row_side, pts, vec):
    first, count = slots
    group_of = lax.broadcasted_iota(jnp.int32, (16, 128), 1) // 32
    outs = [jnp.zeros((16, 128), F) for _ in range(3)]
    for k in range(count):
        rem = src[first + k, 48:64, :]
        for q in range(3):
            turn = (32 * (k - q)) % 128
            outs[q] = jnp.where(group_of == k, pltpu.roll(rem, turn, 1) if turn else rem, outs[q])
    put(chunk, outs[0], jnp.concatenate(outs[1:], axis=0), row_side, pts, vec)


def finish_main(acc, slots, chunk0, out):
    first, count = slots
    for k in range(count):
        c = lanes(chunk0 + k)
        out[first + k, 0:32, :] = (acc[0:32, c] + acc[32:64, c]) * GAIN


def finish_rest(acc, slots, rest, out):
    first, count = slots
    group_of = lax.broadcasted_iota(jnp.int32, (8, 128), 1) // 32
    c = lanes(rest)
    t = (acc[0:32, c] + acc[32:64, c]) * GAIN
    for k in range(count):
        o = jnp.zeros((8, 128), F)
        for q in range(4):
            turn = (32 * (q - k)) % 128
            piece = t[8 * q : 8 * q + 8, :]
            o = jnp.where(group_of == q, pltpu.roll(piece, turn, 1) if turn else piece, o)
        out[first + k, 32:40, :] = o


def block_of(m):
    def pick(cond, yes, no):
        return jnp.where(cond, yes, no)

    third = pick(m >= 6, 2, pick(m >= 3, 1, 0))
    pair = lax.shift_right_logical(jnp.maximum(m - 20, 0), 1)
    j = pick(m < 9, third, pick(m < 12, m - 9, pick(m < 15, m - 12, pick(m < 20, 3, m - 16 - 2 * pair))))
    i = pick(m < 9, m - 3 * third, pick(m < 12, 3, pick(m < 15, 4, pick(m < 20, m - 15, 4 - pair))))
    return j, i


STEPS = 30


def products(A, vj, B, vi, acc_i, acc_j, d, k, actions):
    def place(block, q):
        j, i = block
        return (
            pl.ds(pl.multiple_of((2 * j + q // 2) * TILE, TILE), TILE),
            pl.ds(pl.multiple_of((2 * i + q % 2) * TILE, TILE), TILE),
        )

    def distances(block, q):
        sj, si = place(block, q)
        d[q][...] = jnp.dot(A[sj, :], B[:, si], preferred_element_type=F)

    def kernel_values(q):
        x = jnp.maximum(d[q][...], TINY)
        u = (-ALPHA) - x * lax.rsqrt(x)
        value = (u * u + BETA) * jnp.exp2(u)
        high = value.astype(H)
        k[q][0] = high
        k[q][1] = (value - high.astype(F)).astype(H)

    def accumulate(block, q):
        sj, si = place(block, q)
        v_j, v_i = vj[:, sj], vi[:, si]
        acc_i[:, si] += jnp.dot(
            jnp.concatenate([v_j, v_j], axis=1), jnp.concatenate([k[q][0], k[q][1]], axis=0), preferred_element_type=F
        )
        acc_j[:, sj] += jnp.dot(
            jnp.concatenate([v_i, v_i], axis=1), jnp.concatenate([k[q][0].T, k[q][1].T], axis=0), preferred_element_type=F
        )

    for q in range(3):
        distances(block_of(jnp.int32(0)), q)
    for q in range(1, 4):
        k[q][...] = jnp.zeros_like(k[q])

    def step(m, blocks):
        for at, action in actions.items():
            if at < STEPS:
                pl.when(m == at)(action)
        before, now, after = blocks
        for q in range(4):
            distances(after if q else now, (q + 3) % 4)
            accumulate(before if q < 3 else now, (q + 1) % 4)
            kernel_values(q)
        return now, after, block_of(jnp.minimum(m + 2, STEPS - 1))

    start = block_of(jnp.int32(0))
    lax.fori_loop(0, STEPS, step, (start, start, block_of(jnp.int32(1))))
    actions[STEPS]()
    for q in range(1, 4):
        accumulate(block_of(jnp.int32(STEPS - 1)), q)


def solve_kernel(p_hbm, v_hbm, l_ref, out_ref, p_ref, v_ref, R, C, B, vi, A, vj, acc_i, acc_j, d0, d1, d2, d3, k0, k1, k2, k3,
                 oi, oj, gi, gj, io, rs, rr, cs, cr, ris, rir, cjs, cjr):
    b, r = lax.axis_index("blk"), lax.axis_index("rep")
    core, z, x = lax.rem(b, 2), lax.div(b, 8), lax.rem(r, 4)
    y = lax.div(r, 4) * 4 + lax.rem(lax.div(b, 2), 4)

    def at(dx=0, dy=0, dz=0, dc=0):
        xx, yy, zz = lax.rem(x + dx + 4, 4), lax.rem(y + dy + 8, 8), lax.rem(z + dz + 8, 8)
        cc = 1 - core if dc else core
        return ((zz * 4 + lax.rem(yy, 4)) * 2 + cc, lax.div(yy, 4) * 4 + xx)

    barrier = pltpu.get_barrier_semaphore()
    near = [at(dc=1)] + [at(dz=k) for k in range(1, 8)] + [at(dy=k) for k in range(1, 8)] + [at(dx=k) for k in range(1, 4)]
    for d in near:
        pl.semaphore_signal(barrier, inc=1, device_id=d, device_id_type=pl.DeviceIdType.MESH)
    loads = [pltpu.make_async_copy(p_hbm, p_ref, io.at[0]), pltpu.make_async_copy(v_hbm, v_ref, io.at[1])]
    for t in loads:
        t.start()
    feature = lax.broadcasted_iota(jnp.int32, (16, 160), 0)
    scale = jnp.ones((16, 160), F)
    for f in range(16):
        scale = jnp.where(feature == f, l_ref[f], scale)
    acc_i[...] = jnp.zeros_like(acc_i)
    acc_j[...] = jnp.zeros_like(acc_j)
    pad = pl.ds(NJ - 128, 128)
    A[pad, :] = jnp.zeros((128, 128), H)
    vj[:, pad] = jnp.zeros((64, 128), H)
    for t in loads:
        t.wait()

    own = R.at[0]
    scaled = p_ref[...] / scale * SCALE
    R[0, 0:16, :] = scaled[:, 0:128]
    R[0, 16:48, :] = v_ref[:, 0:128]
    R[0, 48:64, 0:32] = scaled[:, 128:160]
    R[0, 48:64, 32:64] = v_ref[0:16, 128:160]
    R[0, 48:64, 64:96] = v_ref[16:32, 128:160]
    R[0, 48:64, 96:128] = jnp.zeros((16, 32), F)
    C[NSYM] = R[0]
    pl.semaphore_wait(barrier, len(near))

    def send(source, dest, ss, rsem, where):
        return pltpu.make_async_remote_copy(
            src_ref=source, dst_ref=dest, send_sem=ss, recv_sem=rsem, device_id=where,
            device_id_type=pl.DeviceIdType.MESH,
        )

    row, col = {}, {}
    rslot = {dz: 2 * k for k, dz in enumerate(ROWS)}
    for dz in range(8):
        for dc in range(2):
            s = rslot[dz] + dc
            if s == 0:
                continue
            if dc:
                source, where = R.at[rslot[dz]], at(dc=1)
            elif dz == 4:
                source, where = R.at[rslot[3]], at(dz=-1)
            else:
                source, where = own, at(dz=-dz)
            row[dz, dc] = send(source, R.at[s], rs.at[s], rr.at[s], where)
    slot = {o: k for k, o in enumerate(COLS)}
    for (dx, dy), s in slot.items():
        if (dx, dy) == (0, 0):
            continue
        if dx == 0:
            prev, where = ((0, 3), at(dy=-1)) if dy == 4 else ((0, 0), at(dy=-dy))
        else:
            prev, where = (0, dy), at(dx=-dx)
        source = own if prev == (0, 0) else C.at[slot[prev]]
        col[dx, dy] = send(source, C.at[s], cs.at[s], cr.at[s], where)

    for t in (col[0, 1], row[1, 0], row[7, 0], col[1, 0], row[0, 1], col[0, 2], row[2, 0], row[6, 0], col[2, 0],
              col[0, 3], row[3, 0], row[5, 0]):
        t.start()

    def arrive_row(dz, *then):
        row[dz, 0].wait_recv()
        for t in then:
            row[t, 0].start()
        row[dz, 1].start()

    def arrive_col(o, *then):
        col[o].wait_recv()
        for t in then:
            col[t].start()

    def rows_ready(*offsets):
        for dz in offsets:
            row[dz, 1].wait_recv()

    def prepare_rows(group):
        prepare(R, (4 * group, 4), 4 * group, True, B, vi)

    def prepare_cols(first, count, chunk):
        prepare(C, (first, count), chunk, False, A, vj)

    backs = {}

    def back(key, source, dest, ss, rsem, where):
        backs[key] = send(source, dest, ss, rsem, where)

    for k, (dx, dy) in enumerate(SYM):
        for part, rows in enumerate((pl.ds(0, 32), pl.ds(32, 8))):
            e = 2 * k + part
            back((dx, dy, part), oj.at[k, rows], gj.at[k, rows], cjs.at[e], cjr.at[e], at(dx=dx, dy=dy))
    for dz in range(8):
        for dc in range(2):
            if (dz, dc) != (0, 0):
                s, d = rslot[dz] + dc, rslot[(8 - dz) % 8] + dc
                back((dz, dc), oi.at[s], gi.at[d], ris.at[d], rir.at[d], at(dz=dz, dc=dc))

    def return_rows(group):
        finish_main(acc_i, (4 * group, 4), 4 * group, oi)
        finish_rest(acc_i, (4 * group, 4), NROW + group, oi)
        for k in (2 * group + 1, 2 * group):
            for dc in range(2):
                if (ROWS[k], dc) != (0, 0):
                    backs[ROWS[k], dc].start()

    def return_cols(part, first, count):
        for o in SYM[first : first + count]:
            backs[(*o, part)].start()

    def cols_main():
        finish_main(acc_j, (0, 12), 0, oj)
        return_cols(0, 0, 12)

    def cols_next():
        finish_main(acc_j, (12, 2), 12, oj)
        for g in range(2):
            finish_rest(acc_j, REST[g], NSYM + g, oj)
        return_cols(0, 12, 2)
        return_cols(1, 6, 8)

    def cols_last():
        for g in range(2, 4):
            finish_rest(acc_j, REST[g], NSYM + g, oj)
        return_cols(1, 0, 6)

    arrive_col((0, 1), (1, 1), (-1, 1), (2, 1))
    arrive_row(1)
    arrive_row(7)
    arrive_col((0, 2), (1, 2), (-1, 2), (2, 2))
    arrive_row(2)
    arrive_row(6)
    arrive_col((0, 3), (0, 4), (1, 3), (-1, 3), (2, 3))
    arrive_row(3, 4)
    arrive_row(5)
    arrive_col((1, 0))
    rows_ready(0, 1)
    prepare_rows(0)
    prepare_cols(0, 4, 0)
    rows_ready(7, 2)
    prepare_rows(1)

    def at_1():
        rows_ready(6, 3)
        prepare_rows(2)

    def at_2():
        for o in SYM[4:8]:
            arrive_col(o)
        prepare_cols(4, 4, 4)

    def at_5():
        arrive_col((0, 4), (-1, 4), (2, 4))
        arrive_row(4)
        for o in SYM[8:12]:
            arrive_col(o)
        prepare_cols(8, 4, 8)

    def at_8():
        rows_ready(5, 4)
        prepare_rows(3)

    def at_11():
        for g in range(4):
            prepare_rest(R, (4 * g, 4), NROW + g, True, B, vi)

    def at_14():
        arrive_col((2, 3))
        arrive_col((-1, 4))
        prepare_cols(12, 2, 12)
        for g in range(2):
            prepare_rest(C, REST[g], NSYM + g, False, A, vj)

    def at_19():
        arrive_col((2, 0))
        for g in range(2, 4):
            prepare_rest(C, REST[g], NSYM + g, False, A, vj)
        prepare_cols(NSYM, 2, CHUNK_S)

    def at_20():
        arrive_col((2, 4))
        prepare_cols(NSYM + 2, 2, CHUNK_S + 2)
        prepare_rest(C, (NSYM, 4), CHUNK_S + 4, False, A, vj)

    actions = {
        1: at_1, 2: at_2, 5: at_5, 8: at_8, 11: at_11, 14: at_14, 16: cols_main, 19: at_19, 20: at_20, 21: cols_next,
        25: lambda: return_rows(3),
        27: lambda: return_rows(2),
        29: lambda: return_rows(1),
        STEPS: cols_last,
    }
    products(A, vj, B, vi, acc_i, acc_j, (d0, d1, d2, d3), (k0, k1, k2, k3), actions)
    return_rows(0)

    total = oi[0]
    for k, o in enumerate(SYM):
        backs[(*o, 0)].wait_recv()
        backs[(*o, 1)].wait_recv()
        total = total + gj[k]
    for dz in (*ROWS[:0:-1], 0):
        for dc in range(2):
            if (dz, dc) != (0, 0):
                backs[dz, dc].wait_recv()
                total = total + gi[rslot[(8 - dz) % 8] + dc]
    out_ref[:, 0:128] = total[0:32]
    rem = total[32:40]
    for q in range(4):
        turned = pltpu.roll(rem, (-32 * q) % 128, 1) if q else rem
        out_ref[8 * q : 8 * q + 8, 128:160] = turned[:, 0:32]
    for t in (*row.values(), *col.values(), *backs.values()):
        t.wait_send()


def per_device(points, vectors, lengthscales):
    vmem = pl.BlockSpec(memory_space=pltpu.VMEM)
    dma = pltpu.SemaphoreType.DMA
    return pl.pallas_call(
        solve_kernel,
        out_shape=jax.ShapeDtypeStruct(vectors.shape, F),
        in_specs=[pl.BlockSpec(memory_space=pl.ANY)] * 2 + [pl.BlockSpec(memory_space=pltpu.SMEM)],
        out_specs=vmem,
        scratch_shapes=[
            pltpu.VMEM(points.shape, F),
            pltpu.VMEM(vectors.shape, F),
            pltpu.VMEM((NROW, 64, 128), F),
            pltpu.VMEM((NCOL, 64, 128), F),
            pltpu.VMEM((128, NI), H),
            pltpu.VMEM((64, NI), H),
            pltpu.VMEM((NJ, 128), H),
            pltpu.VMEM((64, NJ), H),
            pltpu.VMEM((64, NI), F),
            pltpu.VMEM((64, NJ), F),
            *[pltpu.VMEM((TILE, TILE), F)] * 4,
            *[pltpu.VMEM((2, TILE, TILE), H)] * 4,
            pltpu.VMEM((NROW, 40, 128), F),
            pltpu.VMEM((NSYM, 40, 128), F),
            pltpu.VMEM((NROW, 40, 128), F),
            pltpu.VMEM((NSYM, 40, 128), F),
            dma((2,)),
            dma((NROW,)), dma((NROW,)), dma((NCOL,)), dma((NCOL,)),
            dma((NROW,)), dma((NROW,)), dma((2 * NSYM,)), dma((2 * NSYM,)),
        ],
        compiler_params=pltpu.CompilerParams(collective_id=0, has_side_effects=True),
        name="solve",
    )(points, vectors, lengthscales)


def solution(mesh):
    return jax.shard_map(
        per_device,
        mesh=mesh,
        in_specs=(P(None, ("blk", "rep")), P(None, ("blk", "rep")), P()),
        out_specs=P(None, ("blk", "rep")),
        check_vma=False,
    )
```
